256 devices in a mesh: src: 16 (over x, y), tgt: 16 (over z, core).
Axes of the slice: x: 4, y: 4, z: 8, core: 2. Of those that a mesh axis runs over, the one named last changes fastest.
Arguments:
- src_codes: bfloat16 [1024, 24576], P('tgt', 'src'), may hold values from -1 to 1
- src_scale: float32 [24576], P('src'), may hold values from 0.8 to 1.25
- tgt_codes: bfloat16 [1024, 16384], P('src', 'tgt'), may hold values from -1 to 1
- tgt_scale: float32 [16384], P('tgt'), may hold values from 0.8 to 1.25
Outputs:
- forward_best: float32 [4, 24576], P(None, 'src')
- backward_best: float32 [4, 16384], P(None, 'tgt')
The draws below stay inside these ranges and needn't reach their ends.
All inputs are finite; a program needn't handle non-finite values.
Results may differ from the reference program's by a relative error of at most 0.0003.
Values may be sent and summed in bfloat16 or wider, within the bound.
A program may use at most 64 MiB of HBM per device.

```python
import math
import jax
import jax.numpy as jnp
from jax import lax

D = 1024
KNN = 4
KEEP = 4
NS = 24576
NT = 16384


def rough_noise(key, extent):
    return jnp.clip(0.25 * jax.random.normal(key, extent, jnp.float32), -1.0, 1.0)


def unit_noise(key, extent):
    return jnp.clip(jax.random.normal(key, extent, jnp.float32), -2.0, 2.0)


def shared_direction(key):
    return unit_noise(jax.random.fold_in(key, 21), (D,))


def target_groups(key):
    return rough_noise(jax.random.fold_in(key, 11), (D, NT // 4))


def hub_flags(key):
    groups = NT // 4
    slot = jax.random.randint(jax.random.fold_in(key, 22), (groups // 16 + 1,), 0, 16)
    places = jnp.arange(groups, dtype=jnp.int32)
    return jnp.where(places % 16 == jnp.take(slot, places // 16), 1.0, 0.0).astype(jnp.float32)


def draw_tgt_codes(key, part):
    bases = target_groups(key)
    shared = shared_direction(key)
    member = jnp.arange(NT, dtype=jnp.int32) // 4
    copies = 0.04 * unit_noise(jax.random.fold_in(key, 23), (D, NT))
    hubs = jnp.take(hub_flags(key), member)
    columns = jnp.take(bases, member, axis=1) + copies + 0.25 * hubs[None, :] * shared[:, None]
    return jnp.clip(columns, -1.0, 1.0).astype(jnp.bfloat16)


def draw_src_codes(key, part):
    groups = NS // 4
    bases = target_groups(key)
    shared = shared_direction(key)
    partner = jax.random.randint(jax.random.fold_in(key, 12), (groups,), 0, NT // 4)
    paired = jax.random.randint(jax.random.fold_in(key, 13), (groups,), 0, 2)
    strength = jax.random.uniform(jax.random.fold_in(key, 14), (groups,), jnp.float32, 0.45, 0.85)
    strong = jax.random.randint(jax.random.fold_in(key, 24), (groups,), 0, 32)
    weight = jnp.where(strong == 0, 0.3, 0.05).astype(jnp.float32)
    source_noise = rough_noise(jax.random.fold_in(key, 15), (D, groups))
    blended = strength[None, :] * jnp.take(bases, partner, axis=1) + jnp.sqrt(1.0 - strength * strength)[None, :] * source_noise
    chosen = jnp.where(paired[None, :] == 1, blended, source_noise)
    member = jnp.arange(NS, dtype=jnp.int32) // 4
    copies = 0.04 * unit_noise(jax.random.fold_in(key, 25), (D, NS))
    columns = jnp.take(chosen, member, axis=1) + copies + jnp.take(weight, member)[None, :] * shared[:, None]
    return jnp.clip(columns, -1.0, 1.0).astype(jnp.bfloat16)


def levels(own_key, shape, pieces, least, top_value):
    def one(position, blocks):
        heights = jax.random.uniform(jax.random.fold_in(jax.random.fold_in(own_key, 6), position), (blocks,), jnp.float32, least / len(pieces), top_value / len(pieces))
        return jnp.repeat(jnp.exp(heights), shape[position] // blocks).reshape((-1,) + (1,) * (len(shape) - position - 1))

    gain = one(*pieces[0])
    for cut in pieces[1:]:
        gain = gain * one(*cut)
    return gain


def setup_inputs(seed: int = 0) -> dict:
    key_list = jax.random.split(jax.random.key(seed), 5)
    return {
        "src_codes": draw_src_codes(jax.random.fold_in(key_list[4], 71), 0),
        "src_scale": jnp.clip(jnp.exp(math.log(1.25) - 0.4462871 * jax.random.uniform(key_list[1], (NS,), jnp.float32) ** levels(key_list[1], (NS,), ((0, 16),), -0.2, 0.2)), 0.8, 1.25),
        "tgt_codes": draw_tgt_codes(jax.random.fold_in(key_list[4], 71), 0),
        "tgt_scale": jnp.clip(jnp.exp(math.log(1.25) - 0.4462871 * jax.random.uniform(key_list[3], (NT,), jnp.float32) ** levels(key_list[3], (NT,), ((0, 16),), -0.2, 0.2)), 0.8, 1.25),
    }


def tile_scores(block, block_scale, targets, target_scale):
    dots = lax.dot_general(block, targets, (((0,), (0,)), ((), ())), preferred_element_type=jnp.float32)
    return dots * block_scale[:, None] * target_scale[None, :]


def merge_lists(first, second):
    return lax.top_k(jnp.concatenate([first, second], axis=1), first.shape[1])[0]


def sweep(sources, source_scale, targets, target_scale, source_denom, target_denom, use_margin, width):
    rows = sources.shape[1]
    step = 512 if rows % 512 == 0 else rows
    count = rows // step
    items = (jnp.arange(count, dtype=jnp.int32), source_scale.reshape(count, step), source_denom.reshape(count, step))

    def visit(carry, item):
        index, scale, denom = item
        block = lax.dynamic_slice_in_dim(sources, (index * step).astype(jnp.int32), step, 1)
        sim = tile_scores(block, scale, targets, target_scale)
        if use_margin:
            sim = sim / (0.5 * (denom[:, None] + target_denom[None, :]))
        ahead = lax.top_k(sim, width)[0]
        column = lax.top_k(sim.T, width)[0]
        return merge_lists(carry, column), ahead

    start = jnp.full((targets.shape[1], width), -1e30, jnp.float32)
    behind, ahead = lax.scan(visit, start, items)
    return ahead.reshape(rows, width), behind


def reference(src_codes, src_scale, tgt_codes, tgt_scale):
    dummy_src = jnp.ones_like(src_scale)
    dummy_tgt = jnp.ones_like(tgt_scale)
    ahead, behind = sweep(src_codes, src_scale, tgt_codes, tgt_scale, dummy_src, dummy_tgt, False, KNN)
    forward_knn = jnp.mean(ahead, axis=1)
    backward_knn = jnp.mean(behind, axis=1)
    best_ahead, best_behind = sweep(src_codes, src_scale, tgt_codes, tgt_scale, forward_knn, backward_knn, True, KEEP)
    return best_ahead.T, best_behind.T
```

```python
import functools

import jax
import jax.numpy as jnp
from jax import lax
from jax.experimental import pallas as pl
from jax.experimental.pallas import tpu as pltpu
from jax.sharding import PartitionSpec as P

MESH = pl.DeviceIdType.MESH
F32 = jnp.float32
LOW = -1e30

NX, NY, NZ = 4, 4, 8
GROUP = 16
LANES = 128


def compare(a, b):
    return jnp.maximum(a, b), jnp.minimum(a, b)


def sort4(v):
    a, b = compare(v[0], v[1])
    c, d = compare(v[2], v[3])
    a, c = compare(a, c)
    b, d = compare(b, d)
    b, c = compare(b, c)
    return [a, b, c, d]


def merge4(p, q):
    a, b, c, d = [jnp.maximum(p[i], q[3 - i]) for i in range(4)]
    a, c = compare(a, c)
    b, d = compare(b, d)
    a, b = compare(a, b)
    c, d = compare(c, d)
    return [a, b, c, d]


def tree(lists):
    while len(lists) > 1:
        lists = [merge4(lists[i], lists[i + 1]) for i in range(0, len(lists), 2)]
    return lists[0]


def over_sublanes(best):
    for shift in (4, 2, 1):
        best = merge4(best, [pltpu.roll(v, shift, 0) for v in best])
    return best


def kernel(
    src_ref, src_scale, tgt_ref, tgt_scale, fwd_ref, bwd_ref,
    s_all, t_all, sim, side, lists, columns,
    row_out, row_in, row_mean, row_best,
    col_out, col_in, col_mean, col_best,
    own_sem, z_send, z_recv, d_send, d_recv, p_send, p_recv,
    g_send, g_recv, h_send, h_recv,
):
    src_me, tgt_me = lax.axis_index("src"), lax.axis_index("tgt")
    x, y = src_me // NY, lax.rem(src_me, NY)
    z, core = tgt_me // 2, lax.rem(tgt_me, 2)
    row_blocks, col_blocks = row_out.shape[0], col_out.shape[0]

    def around(v, step, n):
        return lax.rem(v + (step + n), n)

    def at_xy(dx, dy):
        return around(x, dx, NX) * NY + around(y, dy, NY)

    def at_z(dz):
        return around(z, dz, NZ) * 2 + core

    barrier = pltpu.get_barrier_semaphore()
    for r in range(1, GROUP):
        pl.semaphore_signal(
            barrier, inc=1, device_id=(src_me, around(tgt_me, r, GROUP)), device_id_type=MESH
        )
        pl.semaphore_signal(
            barrier, inc=1, device_id=(around(src_me, r, GROUP), tgt_me), device_id_type=MESH
        )

    own = []
    for h in range(2):
        part = pl.ds(h * 32, 32)
        own.append(pltpu.make_async_copy(src_ref.at[part], s_all.at[tgt_me, h], own_sem.at[0, h]))
        own.append(pltpu.make_async_copy(tgt_ref.at[part], t_all.at[src_me, h], own_sem.at[1, h]))
    for copy in own:
        copy.start()

    for b in range(row_blocks):
        line = src_scale[:, b * LANES:(b + 1) * LANES]
        side[b * LANES:(b + 1) * LANES, :] = jnp.broadcast_to(line, (LANES, LANES)).T
    columns[...] = jnp.full(columns.shape, LOW, F32)
    for copy in own:
        copy.wait()
    pl.semaphore_wait(barrier, 2 * (GROUP - 1))

    sent = []

    def z_copy(way, d, h):
        step = 1 if way == 0 else -1
        slot = s_all.at[at_z(-step * (d - 1)), h]
        return pltpu.make_async_remote_copy(
            src_ref=slot, dst_ref=slot,
            send_sem=z_send.at[way, d - 1, h], recv_sem=z_recv.at[way, d - 1, h],
            device_id=(src_me, at_z(step)), device_id_type=MESH,
        )

    def z_landed(way, d, h):
        step = 1 if way == 0 else -1
        slot = s_all.at[at_z(-step * d), h]
        pltpu.make_async_remote_copy(
            src_ref=slot, dst_ref=slot,
            send_sem=z_send.at[way, d - 1, h], recv_sem=z_recv.at[way, d - 1, h],
            device_id=(src_me, at_z(step)), device_id_type=MESH,
        ).wait_recv()

    def sibling(dz, h, wait=False):
        there = around(z, dz, NZ) * 2 + (1 - core if wait else core)
        slot = s_all.at[there, h]
        copy = pltpu.make_async_remote_copy(
            src_ref=slot, dst_ref=slot,
            send_sem=d_send.at[dz % NZ, h], recv_sem=d_recv.at[dz % NZ, h],
            device_id=(src_me, z * 2 + 1 - core), device_id_type=MESH,
        )
        if wait:
            copy.wait_recv()
        else:
            go(copy)

    def go(copy):
        copy.start()
        sent.append(copy)

    def z_event(d, h):
        for way in range(2):
            if d == NZ // 2 and h != way:
                continue
            z_landed(way, d, h)
            if d < NZ // 2 - 1 or (d == NZ // 2 - 1 and h == way):
                go(z_copy(way, d + 1, h))
            sibling(-d if way == 0 else d, h)

    def place(h, first, second):
        return at_xy(first, second) if h == 0 else at_xy(second, first)

    moves = ((1, 0), (-1, 0), (0, 1), (0, -1))

    def p_copy(h, index, slice_at, move):
        slot = t_all.at[place(h, *slice_at), h]
        go(pltpu.make_async_remote_copy(
            src_ref=slot, dst_ref=slot,
            send_sem=p_send.at[h, index], recv_sem=p_recv.at[h, index],
            device_id=(place(h, *moves[move]), tgt_me), device_id_type=MESH,
        ))

    def p_landed(h, index, slice_at):
        slot = t_all.at[place(h, *slice_at), h]
        pltpu.make_async_remote_copy(
            src_ref=slot, dst_ref=slot,
            send_sem=p_send.at[h, index], recv_sem=p_recv.at[h, index],
            device_id=(src_me, tgt_me), device_id_type=MESH,
        ).wait_recv()

    offsets = (0, -1, 1, 2)

    def p_second(h, j):
        p_copy(h, 3 + 3 * j, (offsets[j], 0), 2)
        p_copy(h, 4 + 3 * j, (offsets[j], 0), 3)

    def p_own():
        for h in range(2):
            p_copy(h, 0, (0, 0), 0)
            p_copy(h, 1, (0, 0), 1)
            p_second(h, 0)

    def p_first():
        for h in range(2):
            p_landed(h, 0, (-1, 0))
            p_copy(h, 2, (-1, 0), 0)
            p_second(h, 1)
        for h in range(2):
            p_landed(h, 1, (1, 0))
            p_second(h, 2)

    def p_opposite():
        for h in range(2):
            p_landed(h, 2, (-2, 0))
            p_second(h, 3)

    def p_lines(j):
        up = j in (0, 3)
        for h in range(2):
            p_landed(h, 3 + 3 * j, (offsets[j], -1))
            if up:
                p_copy(h, 5 + 3 * j, (offsets[j], -1), 2)
        for h in range(2):
            p_landed(h, 4 + 3 * j, (offsets[j], 1))
            if not up:
                p_copy(h, 5 + 3 * j, (offsets[j], 1), 3)

    def p_last():
        for j in range(4):
            for h in range(2):
                p_landed(h, 5 + 3 * j, (offsets[j], 2))

    for h in range(2):
        go(z_copy(0, 1, h))
        go(z_copy(1, 1, h))
    p_own()
    for h in range(2):
        sibling(0, h)
    p_first()
    z_event(1, 0)
    p_lines(0)
    z_event(1, 1)
    p_opposite()
    p_lines(1)
    z_event(2, 0)
    p_lines(2)
    z_event(2, 1)
    p_lines(3)
    z_event(3, 0)
    p_last()
    z_event(3, 1)
    z_event(4, 0)
    z_event(4, 1)
    for dz in range(NZ):
        for h in range(2):
            sibling(dz, h, wait=True)
    for copy in sent:
        copy.wait_send()

    depth = s_all.shape[0] * s_all.shape[1] * s_all.shape[2]
    tile = 256

    @pl.loop(0, sim.shape[0] // tile)
    def _(i):
        part = pl.ds(pl.multiple_of(i * tile, tile), tile)
        left = s_all[:, :, :, part].reshape(depth, tile)
        right = t_all[...].reshape(depth, sim.shape[1])
        sim[part, :] = lax.dot_general(
            left, right, (((0,), (0,)), ((), ())), preferred_element_type=F32
        )

    def sweep(change):
        @pl.loop(0, row_blocks)
        def _(b):
            def rows(g):
                return pl.ds(pl.multiple_of(b * LANES + g * 8, 8), 8)

            for g in range(16):
                beside = side[rows(g), :]
                values = []
                for c in range(col_blocks):
                    lane = pl.ds(c * LANES, LANES)
                    value = change(sim[rows(g), lane], beside, c)
                    sim[rows(g), lane] = value
                    values.append(value)
                best = merge4(sort4(values[:4]), sort4(values[4:]))
                for k in range(4):
                    lists[k, g * 8:(g + 1) * 8, :] = best[k]
            turned = [lists[k].T for k in range(4)]
            best = over_sublanes(tree([[t[g * 8:(g + 1) * 8] for t in turned] for g in range(16)]))
            for k in range(4):
                row_out[b, k:k + 1, :] = best[k][0:1]
            for c in range(col_blocks):
                lane = pl.ds(c * LANES, LANES)
                quads = [
                    sort4([sim[rows(4 * q + g), lane] for g in range(4)]) for q in range(4)
                ]
                best = merge4(tree(quads), [columns[c, k] for k in range(4)])
                for k in range(4):
                    columns[c, k] = best[k]

        for c in range(col_blocks):
            best = over_sublanes([columns[c, k] for k in range(4)])
            for k in range(4):
                col_out[c, k:k + 1, :] = best[k][0:1]

    axes = (
        (0, tgt_me, row_blocks, row_out, row_in, lambda v: (src_me, v)),
        (1, src_me, col_blocks, col_out, col_in, lambda v: (v, tgt_me)),
    )

    def exchange(stage, results, finish):
        def hand(a, me, blocks, out, into, device, r):
            to = around(me, r, GROUP)
            return pltpu.make_async_remote_copy(
                src_ref=out.at[lax.rem(to, blocks)], dst_ref=into.at[stage, me],
                send_sem=g_send.at[stage, a, r], recv_sem=g_recv.at[stage, a, r],
                device_id=device(to), device_id_type=MESH,
            ), to

        def share(a, me, result, device, r):
            return pltpu.make_async_remote_copy(
                src_ref=result.at[me], dst_ref=result.at[me],
                send_sem=h_send.at[stage, a, r], recv_sem=h_recv.at[stage, a, me],
                device_id=device(around(me, r, GROUP)), device_id_type=MESH,
            )

        for a, me, blocks, out, into, device in axes:
            for r in range(1, GROUP):
                copy, to = hand(a, me, blocks, out, into, device, r)

                @pl.when(to < blocks)
                def _(copy=copy):
                    copy.start()

        for (a, me, blocks, out, into, device), result in zip(axes, results):
            @pl.when(me < blocks)
            def _(a=a, me=me, blocks=blocks, out=out, into=into, device=device, result=result):
                into[stage, me] = out[me]
                for r in range(1, GROUP):
                    pltpu.make_async_remote_copy(
                        src_ref=out.at[0], dst_ref=into.at[stage, around(me, -r, GROUP)],
                        send_sem=g_send.at[stage, a, r], recv_sem=g_recv.at[stage, a, r],
                        device_id=device(me), device_id_type=MESH,
                    ).wait_recv()
                halves = [[into[stage, pl.ds(p, 8), k, :] for k in range(4)] for p in (0, 8)]
                finish(result, me, over_sublanes(merge4(*halves)))
                for r in range(1, GROUP):
                    share(a, me, result, device, r).start()

        for (a, me, blocks, out, into, device), result in zip(axes, results):
            for b in range(blocks):
                @pl.when(me != b)
                def _(b=b, a=a, device=device, result=result, me=me):
                    pltpu.make_async_remote_copy(
                        src_ref=result.at[b], dst_ref=result.at[b],
                        send_sem=h_send.at[stage, a, 0], recv_sem=h_recv.at[stage, a, b],
                        device_id=device(me), device_id_type=MESH,
                    ).wait_recv()

        for (a, me, blocks, out, into, device), result in zip(axes, results):
            for r in range(1, GROUP):
                copy, to = hand(a, me, blocks, out, into, device, r)

                @pl.when(to < blocks)
                def _(copy=copy):
                    copy.wait_send()

            @pl.when(me < blocks)
            def _(a=a, me=me, device=device, result=result):
                for r in range(1, GROUP):
                    share(a, me, result, device, r).wait_send()

    def scaled(value, beside, c):
        return value * beside * tgt_scale[:, c * LANES:(c + 1) * LANES]

    def half_mean(result, me, best):
        result[me] = (best[0] + best[1] + best[2] + best[3]) * 0.125

    sweep(scaled)
    exchange(0, (row_mean, col_mean), half_mean)

    for b in range(row_blocks):
        line = row_mean[b]
        side[b * LANES:(b + 1) * LANES, :] = jnp.concatenate([line] * 16, axis=0).T
    columns[...] = jnp.full(columns.shape, LOW, F32)

    def margin(value, beside, c):
        return value / (beside + col_mean[c])

    def keep(result, me, best):
        for k in range(4):
            result[me, k:k + 1, :] = best[k][0:1]

    sweep(margin)
    exchange(1, (row_best, col_best), keep)

    for b in range(row_blocks):
        fwd_ref[:, b * LANES:(b + 1) * LANES] = row_best[b, 0:4, :]
    for c in range(col_blocks):
        bwd_ref[:, c * LANES:(c + 1) * LANES] = col_best[c, 0:4, :]


def body(src_codes, src_scale, tgt_codes, tgt_scale):
    depth, rows = src_codes.shape
    cols = tgt_codes.shape[1]
    row_blocks, col_blocks = rows // LANES, cols // LANES
    vmem = pl.BlockSpec(memory_space=pltpu.VMEM)
    hbm = pl.BlockSpec(memory_space=pl.ANY)
    dma = pltpu.SemaphoreType.DMA
    return pl.pallas_call(
        kernel,
        out_shape=(
            jax.ShapeDtypeStruct((4, rows), F32),
            jax.ShapeDtypeStruct((4, cols), F32),
        ),
        in_specs=[hbm, vmem, hbm, vmem],
        out_specs=(vmem, vmem),
        scratch_shapes=[
            pltpu.VMEM((GROUP, 2, depth // 2, rows), jnp.bfloat16),
            pltpu.VMEM((GROUP, 2, depth // 2, cols), jnp.bfloat16),
            pltpu.VMEM((rows, cols), F32),
            pltpu.VMEM((rows, LANES), F32),
            pltpu.VMEM((4, LANES, LANES), F32),
            pltpu.VMEM((col_blocks, 4, 8, LANES), F32),
            pltpu.VMEM((row_blocks, 8, LANES), F32),
            pltpu.VMEM((2, GROUP, 8, LANES), F32),
            pltpu.VMEM((row_blocks, 8, LANES), F32),
            pltpu.VMEM((row_blocks, 8, LANES), F32),
            pltpu.VMEM((col_blocks, 8, LANES), F32),
            pltpu.VMEM((2, GROUP, 8, LANES), F32),
            pltpu.VMEM((col_blocks, 8, LANES), F32),
            pltpu.VMEM((col_blocks, 8, LANES), F32),
            dma((2, 2)),
            dma((2, NZ // 2, 2)),
            dma((2, NZ // 2, 2)),
            dma((NZ, 2)),
            dma((NZ, 2)),
            dma((2, 15)),
            dma((2, 15)),
            dma((2, 2, GROUP)),
            dma((2, 2, GROUP)),
            dma((2, 2, GROUP)),
            dma((2, 2, GROUP)),
        ],
        compiler_params=pltpu.CompilerParams(
            collective_id=0, has_side_effects=True, vmem_limit_bytes=40 * 1024 * 1024
        ),
        name="mine",
    )(src_codes, src_scale.reshape(1, rows), tgt_codes, tgt_scale.reshape(1, cols))


def solution(mesh):
    placed = (P("tgt", "src"), P("src"), P("src", "tgt"), P("tgt"))
    return jax.shard_map(
        body,
        mesh=mesh,
        in_specs=placed,
        out_specs=(P(None, "src"), P(None, "tgt")),
        check_vma=False,
    )
```

```python
import jax
import jax.numpy as jnp
from jax import lax
from jax.experimental import pallas as pl
from jax.experimental.pallas import tpu as pltpu
from jax.sharding import PartitionSpec as P

MESH = pl.DeviceIdType.MESH
F32 = jnp.float32
LOW = -1e30

NX, NY, NZ = 4, 4, 8
GROUP = 16
LANES = 128
PIECES = 4
TILE = 256


def compare(a, b):
    return jnp.maximum(a, b), jnp.minimum(a, b)


def sort4(v):
    a, b = compare(v[0], v[1])
    c, d = compare(v[2], v[3])
    a, c = compare(a, c)
    b, d = compare(b, d)
    b, c = compare(b, c)
    return [a, b, c, d]


def merge4(p, q):
    a, b, c, d = [jnp.maximum(p[i], q[3 - i]) for i in range(4)]
    a, c = compare(a, c)
    b, d = compare(b, d)
    a, b = compare(a, b)
    c, d = compare(c, d)
    return [a, b, c, d]


def tree(lists):
    while len(lists) > 1:
        odd = lists[len(lists) // 2 * 2:]
        lists = [merge4(lists[i], lists[i + 1]) for i in range(0, len(lists) - 1, 2)] + odd
    return lists[0]


def over_sublanes(best):
    for shift in (4, 2, 1):
        best = merge4(best, [pltpu.roll(v, shift, 0) for v in best])
    return best


TAIL = (32, 40, 44, 36)


def row_line(k, b):
    return jnp.where(b < 8, 8 * k + b, TAIL[k] + b - 8)


def load_rows(ref):
    head = [ref[8 * k:8 * k + 8, :] for k in range(4)]
    first, second = ref[32:40, :], ref[40:48, :]
    return head, [first, second, pltpu.roll(second, 4, 0), pltpu.roll(first, 4, 0)]


def kernel(
    src_ref, src_scale, tgt_ref, tgt_scale, fwd_ref, bwd_ref,
    s_all, t_all, sim, side, lists, columns,
    row_out, row_in, pair_out, pair_in,
    col_out, col_in, col_mean,
    own_sem, z_send, z_recv, d_send, d_recv, p_send, p_recv, p_rest,
    x_send, x_recv,
):
    src_me, tgt_me = lax.axis_index("src"), lax.axis_index("tgt")
    x, y = src_me // NY, lax.rem(src_me, NY)
    z, core = tgt_me // 2, lax.rem(tgt_me, 2)
    row_blocks, col_blocks = sim.shape[0] // LANES, sim.shape[1] // LANES

    def around(v, step, n):
        return lax.rem(v + (step + n), n)

    def at_xy(dx, dy):
        return around(x, dx, NX) * NY + around(y, dy, NY)

    def at_z(dz):
        return around(z, dz, NZ) * 2 + core

    twin = (src_me, z * 2 + 1 - core)

    barrier = pltpu.get_barrier_semaphore()
    neighbours = [(src_me, at_z(1)), (src_me, at_z(-1)), twin]
    neighbours += [(at_xy(*move), tgt_me) for move in ((1, 0), (-1, 0), (0, 1), (0, -1))]
    for device in neighbours:
        pl.semaphore_signal(barrier, inc=1, device_id=device, device_id_type=MESH)

    own = []
    for h in range(PIECES):
        part = pl.ds(h * 16, 16)
        own.append(pltpu.make_async_copy(src_ref.at[part], s_all.at[tgt_me, h], own_sem.at[0, h]))
    for h in range(2):
        part = pl.ds(h * 32, 32)
        own.append(pltpu.make_async_copy(tgt_ref.at[part], t_all.at[src_me, h], own_sem.at[1, h]))
    for copy in own:
        copy.start()

    for copy in own:
        copy.wait()
    pl.semaphore_wait(barrier, len(neighbours))

    def z_copy(way, d, h, landed=False):
        step = 1 if way == 0 else -1
        slot = s_all.at[at_z(-step * (d if landed else d - 1)), h]
        return pltpu.make_async_remote_copy(
            src_ref=slot, dst_ref=slot,
            send_sem=z_send, recv_sem=z_recv.at[way, d - 1, h],
            device_id=(src_me, at_z(step)), device_id_type=MESH,
        )

    def goes(way, d, h):
        return d < NZ // 2 or (d == NZ // 2 and (h < PIECES // 2) == (way == 0))

    def to_twin(dz, h):
        slot = s_all.at[at_z(dz), h]
        pltpu.make_async_remote_copy(
            src_ref=slot, dst_ref=slot, send_sem=d_send, recv_sem=d_recv.at[dz % NZ],
            device_id=twin, device_id_type=MESH,
        ).start()

    def from_twin(dz):
        slot = s_all.at[around(z, dz, NZ) * 2 + 1 - core]
        pltpu.make_async_remote_copy(
            src_ref=slot, dst_ref=slot, send_sem=d_send, recv_sem=d_recv.at[dz % NZ],
            device_id=twin, device_id_type=MESH,
        ).wait_recv()

    def z_event(d, h):
        for way in range(2):
            if goes(way, d, h):
                z_copy(way, d, h, landed=True).wait_recv()
                if goes(way, d + 1, h):
                    z_copy(way, d + 1, h).start()
                to_twin(-d if way == 0 else d, h)

    def place(h, first, second):
        return at_xy(first, second) if h == 0 else at_xy(second, first)

    moves = ((1, 0), (-1, 0), (0, 1), (0, -1))

    def p_copy(h, index, slice_at, move):
        slot = t_all.at[place(h, *slice_at), h]
        return pltpu.make_async_remote_copy(
            src_ref=slot, dst_ref=slot,
            send_sem=p_send, recv_sem=p_rest if index is None else p_recv.at[h, index],
            device_id=(place(h, *moves[move]), tgt_me), device_id_type=MESH,
        )

    offsets = (0, -1, 1, 2)
    upward = (True, False, False, True)

    def p_second(h, j):
        p_copy(h, 3 + j if upward[j] else None, (offsets[j], 0), 2).start()
        p_copy(h, None if upward[j] else 3 + j, (offsets[j], 0), 3).start()

    def p_own():
        for h in range(2):
            p_copy(h, 0, (0, 0), 0).start()
            p_copy(h, 1, (0, 0), 1).start()
            p_second(h, 0)

    def p_first():
        for h in range(2):
            p_copy(h, 0, (-1, 0), 0).wait_recv()
            p_copy(h, 2, (-1, 0), 0).start()
            p_second(h, 1)
        for h in range(2):
            p_copy(h, 1, (1, 0), 0).wait_recv()
            p_second(h, 2)

    def p_opposite():
        for h in range(2):
            p_copy(h, 2, (-2, 0), 0).wait_recv()
            p_second(h, 3)

    def p_line(j):
        for h in range(2):
            slice_at = (offsets[j], -1 if upward[j] else 1)
            p_copy(h, 3 + j, slice_at, 2).wait_recv()
            p_copy(h, None, slice_at, 2 if upward[j] else 3).start()

    for h in range(PIECES):
        for way in range(2):
            z_copy(way, 1, h).start()
    p_own()
    for h in range(PIECES):
        to_twin(0, h)

    for b in range(row_blocks):
        line = src_scale[:, b * LANES:(b + 1) * LANES]
        side[b * LANES:(b + 1) * LANES, :] = jnp.broadcast_to(line, (LANES, LANES)).T
    columns[...] = jnp.full(columns.shape, LOW, F32)

    p_first()
    z_event(1, 0)
    p_line(0)
    z_event(1, 1)
    p_opposite()
    z_event(1, 2)
    p_line(1)
    z_event(1, 3)
    z_event(2, 0)
    p_line(2)
    z_event(2, 1)
    p_line(3)
    z_event(2, 2)
    z_event(2, 3)
    pltpu.make_async_copy(t_all.at[pl.ds(0, 8)], t_all.at[pl.ds(0, 8)], p_rest).wait()

    def features(dz, part):
        return s_all[pl.ds(around(z, dz, NZ) * 2, 2), :, :, part].reshape(LANES, TILE)

    def targets(dz):
        return t_all[pl.ds(around(z, dz, NZ) * 2, 2)].reshape(LANES, sim.shape[1])

    def product(first, second, start, stop, fresh=False):
        @pl.loop(start, stop)
        def _(i):
            part = pl.ds(pl.multiple_of(i * TILE, TILE), TILE)
            left = jnp.concatenate([features(first, part), features(second, part)], axis=0)
            right = jnp.concatenate([targets(first), targets(second)], axis=0)
            dots = lax.dot_general(
                left, right, (((0,), (0,)), ((), ())), preferred_element_type=F32
            )
            if fresh:
                sim[part, :] = dots
            else:
                sim[part, :] = sim[part, :] + dots

    tiles = sim.shape[0] // TILE
    half = tiles // 2
    from_twin(-1)
    from_twin(1)
    z_event(3, 0)
    product(-1, 1, 0, half, fresh=True)
    z_event(3, 1)
    product(-1, 1, half, tiles, fresh=True)
    from_twin(-2)
    from_twin(2)
    z_event(3, 2)
    product(-2, 2, 0, half)
    z_event(3, 3)
    product(-2, 2, half, tiles)
    from_twin(-3)
    from_twin(3)
    z_event(4, 0)
    z_event(4, 2)
    product(-3, 3, 0, half)
    z_event(4, 1)
    z_event(4, 3)
    product(-3, 3, half, tiles)
    from_twin(0)
    from_twin(4)
    product(0, 4, 0, tiles)

    for slots, sem in ((s_all.at[pl.ds(0, 7)], z_send), (s_all.at[pl.ds(0, 8)], d_send),
                       (t_all.at[pl.ds(0, 15)], p_send)):
        pltpu.make_async_copy(slots, slots, sem).wait()

    def sweep(change):
        @pl.loop(0, row_blocks)
        def _(b):
            def rows(g):
                return pl.ds(pl.multiple_of(b * LANES + g * 8, 8), 8)

            for g in range(16):
                beside = side[rows(g), :]
                values = []
                for c in range(col_blocks):
                    lane = pl.ds(c * LANES, LANES)
                    value = change(sim[rows(g), lane], beside, c)
                    sim[rows(g), lane] = value
                    values.append(value)
                best = merge4(sort4(values[:4]), sort4(values[4:]))
                for k in range(4):
                    lists[k, g * 8:(g + 1) * 8, :] = best[k]
            turned = [lists[k].T for k in range(4)]
            best = over_sublanes(tree([[t[g * 8:(g + 1) * 8] for t in turned] for g in range(16)]))
            for k in range(4):
                row_out[pl.ds(row_line(k, b), 1), :] = best[k][0:1]
            for c in range(col_blocks):
                lane = pl.ds(c * LANES, LANES)
                quads = [
                    sort4([sim[rows(4 * q + g), lane] for g in range(4)]) for q in range(4)
                ]
                best = merge4(tree(quads), [columns[c, k] for k in range(4)])
                for k in range(4):
                    columns[c, k] = best[k]

        for c in range(col_blocks):
            best = over_sublanes([columns[c, k] for k in range(4)])
            for k in range(4):
                col_out[k, c:c + 1, :] = best[k][0:1]

    def exchange(stage):
        sends = []
        for r in range(1, NZ):
            sends.append(pltpu.make_async_remote_copy(
                src_ref=row_out, dst_ref=row_in.at[stage, r - 1],
                send_sem=x_send.at[0], recv_sem=x_recv.at[stage, 0],
                device_id=(src_me, at_z(r)), device_id_type=MESH,
            ))
        for r in range(1, GROUP):
            sends.append(pltpu.make_async_remote_copy(
                src_ref=col_out, dst_ref=col_in.at[stage, r - 1],
                send_sem=x_send.at[1], recv_sem=x_recv.at[stage, 1],
                device_id=(around(src_me, r, GROUP), tgt_me), device_id_type=MESH,
            ))
        for copy in sends:
            copy.start()
        row_slots, col_slots = row_in.at[stage], col_in.at[stage]

        pltpu.make_async_copy(row_slots, row_slots, x_recv.at[stage, 0]).wait()
        ours = [load_rows(row_out)] + [load_rows(row_in.at[stage, r]) for r in range(NZ - 1)]
        head, tail = tree([v[0] for v in ours]), tree([v[1] for v in ours])
        for k in range(4):
            pair_out[8 * k:8 * k + 8, :] = head[k]
            pair_out[TAIL[k]:TAIL[k] + 4, :] = tail[k][0:4]
        pair = pltpu.make_async_remote_copy(
            src_ref=pair_out, dst_ref=pair_in.at[stage],
            send_sem=x_send.at[2], recv_sem=x_recv.at[stage, 2],
            device_id=twin, device_id_type=MESH,
        )
        pair.start()

        pltpu.make_async_copy(col_slots, col_slots, x_recv.at[stage, 1]).wait()
        everyone = [[col_out[k] for k in range(4)]]
        everyone += [[col_in[stage, r, k] for k in range(4)] for r in range(GROUP - 1)]
        col_best = tree(everyone)

        pair.wait_recv()
        other_head, other_tail = load_rows(pair_in.at[stage])
        head, tail = merge4(head, other_head), merge4(tail, other_tail)
        pair.wait_send()
        pltpu.make_async_copy(row_slots, row_slots, x_send.at[0]).wait()
        pltpu.make_async_copy(col_slots, col_slots, x_send.at[1]).wait()
        return head, tail, col_best

    def line_of(head, tail, b):
        return head[b:b + 1] if b < 8 else tail[b - 8:b - 7]

    def scaled(value, beside, c):
        return value * beside * tgt_scale[:, c * LANES:(c + 1) * LANES]

    def half_mean(best):
        return (best[0] + best[1] + best[2] + best[3]) * 0.125

    sweep(scaled)
    head, tail, col_best = exchange(0)

    head, tail, beneath = half_mean(head), half_mean(tail), half_mean(col_best)
    for b in range(row_blocks):
        line = line_of(head, tail, b)
        side[b * LANES:(b + 1) * LANES, :] = jnp.broadcast_to(line, (LANES, LANES)).T
    for c in range(col_blocks):
        col_mean[c] = jnp.broadcast_to(beneath[c:c + 1], (8, LANES))
    columns[...] = jnp.full(columns.shape, LOW, F32)

    def margin(value, beside, c):
        return value / (beside + col_mean[c])

    sweep(margin)
    head, tail, col_best = exchange(1)
    for k in range(4):
        for b in range(row_blocks):
            fwd_ref[k:k + 1, b * LANES:(b + 1) * LANES] = line_of(head[k], tail[k], b)
        for c in range(col_blocks):
            bwd_ref[k:k + 1, c * LANES:(c + 1) * LANES] = col_best[k][c:c + 1]


def body(src_codes, src_scale, tgt_codes, tgt_scale):
    depth, rows = src_codes.shape
    cols = tgt_codes.shape[1]
    col_blocks = cols // LANES
    vmem = pl.BlockSpec(memory_space=pltpu.VMEM)
    hbm = pl.BlockSpec(memory_space=pltpu.HBM)
    dma = pltpu.SemaphoreType.DMA
    return pl.pallas_call(
        kernel,
        out_shape=(
            jax.ShapeDtypeStruct((4, rows), F32),
            jax.ShapeDtypeStruct((4, cols), F32),
        ),
        in_specs=[hbm, vmem, hbm, vmem],
        out_specs=(vmem, vmem),
        scratch_shapes=[
            pltpu.VMEM((GROUP, PIECES, depth // PIECES, rows), jnp.bfloat16),
            pltpu.VMEM((GROUP, 2, depth // 2, cols), jnp.bfloat16),
            pltpu.VMEM((rows, cols), F32),
            pltpu.VMEM((rows, LANES), F32),
            pltpu.VMEM((4, LANES, LANES), F32),
            pltpu.VMEM((col_blocks, 4, 8, LANES), F32),
            pltpu.VMEM((48, LANES), F32),
            pltpu.VMEM((2, NZ - 1, 48, LANES), F32),
            pltpu.VMEM((48, LANES), F32),
            pltpu.VMEM((2, 48, LANES), F32),
            pltpu.VMEM((4, 8, LANES), F32),
            pltpu.VMEM((2, GROUP - 1, 4, 8, LANES), F32),
            pltpu.VMEM((col_blocks, 8, LANES), F32),
            dma((2, 4)),
            dma,
            dma((2, NZ // 2, PIECES)),
            dma,
            dma((NZ,)),
            dma,
            dma((2, 7)),
            dma,
            dma((3,)),
            dma((2, 3)),
        ],
        compiler_params=pltpu.CompilerParams(
            collective_id=0, has_side_effects=True, vmem_limit_bytes=40 * 1024 * 1024
        ),
        name="mine",
    )(src_codes, src_scale.reshape(1, rows), tgt_codes, tgt_scale.reshape(1, cols))


def solution(mesh):
    placed = (P("tgt", "src"), P("src"), P("src", "tgt"), P("tgt"))
    return jax.shard_map(
        body,
        mesh=mesh,
        in_specs=placed,
        out_specs=(P(None, "src"), P(None, "tgt")),
        check_vma=False,
    )
```

```python
import jax
import jax.numpy as jnp
from jax import lax
from jax.experimental import pallas as pl
from jax.experimental.pallas import tpu as pltpu
from jax.sharding import PartitionSpec as P

MESH = pl.DeviceIdType.MESH
F32 = jnp.float32
LOW = -1e30

NX, NY, NZ = 4, 4, 8
GROUP = 16
LANES = 128
PIECES = 4
QUARTERS = 4
TILE = 1536


def compare(a, b):
    return jnp.maximum(a, b), jnp.minimum(a, b)


def sort4(v):
    a, b = compare(v[0], v[1])
    c, d = compare(v[2], v[3])
    a, c = compare(a, c)
    b, d = compare(b, d)
    b, c = compare(b, c)
    return [a, b, c, d]


def merge4(p, q):
    a, b, c, d = [jnp.maximum(p[i], q[3 - i]) for i in range(4)]
    a, c = compare(a, c)
    b, d = compare(b, d)
    a, b = compare(a, b)
    c, d = compare(c, d)
    return [a, b, c, d]


def tree(lists):
    while len(lists) > 1:
        odd = lists[len(lists) // 2 * 2:]
        lists = [merge4(lists[i], lists[i + 1]) for i in range(0, len(lists) - 1, 2)] + odd
    return lists[0]


def over_sublanes(best):
    for shift in (4, 2, 1):
        best = merge4(best, [pltpu.roll(v, shift, 0) for v in best])
    return best


TAIL = (32, 40, 44, 36)


def row_line(k, b):
    return jnp.where(b < 8, 8 * k + b, TAIL[k] + b - 8)


def load_rows(ref):
    head = [ref[8 * k:8 * k + 8, :] for k in range(4)]
    first, second = ref[32:40, :], ref[40:48, :]
    return head, [first, second, pltpu.roll(second, 4, 0), pltpu.roll(first, 4, 0)]


def kernel(
    src_ref, src_scale, tgt_ref, tgt_scale, fwd_ref, bwd_ref,
    s_all, t_all, sim, side, lists, columns,
    row_out, row_in, pair_out, pair_in,
    col_out, col_in, col_mean,
    own_sem, z_send, z_recv, d_send, d_recv, p_send, p_recv, p_rest,
    x_send, x_recv,
):
    src_me, tgt_me = lax.axis_index("src"), lax.axis_index("tgt")
    x, y = src_me // NY, lax.rem(src_me, NY)
    z, core = tgt_me // 2, lax.rem(tgt_me, 2)
    row_blocks, col_blocks = sim.shape[0] // LANES, sim.shape[1] // LANES

    def around(v, step, n):
        return lax.rem(v + (step + n), n)

    def at_xy(dx, dy):
        return around(x, dx, NX) * NY + around(y, dy, NY)

    def at_z(dz):
        return around(z, dz, NZ) * 2 + core

    twin = (src_me, z * 2 + 1 - core)

    barrier = pltpu.get_barrier_semaphore()
    neighbours = [(src_me, at_z(1)), (src_me, at_z(-1)), twin]
    steps = ((1, 0), (-1, 0), (2, 0), (0, 1), (0, -1), (0, 2))
    neighbours += [(at_xy(*step), tgt_me) for step in steps]
    for device in neighbours:
        pl.semaphore_signal(barrier, inc=1, device_id=device, device_id_type=MESH)

    own = []
    for h in range(PIECES):
        part = pl.ds(h * 16, 16)
        own.append(pltpu.make_async_copy(src_ref.at[part], s_all.at[tgt_me, h], own_sem.at[0, h]))
    for h in range(QUARTERS):
        part = pl.ds(h * 16, 16)
        own.append(pltpu.make_async_copy(tgt_ref.at[part], t_all.at[src_me, h], own_sem.at[1, h]))
    for copy in own:
        copy.start()

    for copy in own:
        copy.wait()
    pl.semaphore_wait(barrier, len(neighbours))

    def z_copy(way, d, h, landed=False):
        step = 1 if way == 0 else -1
        slot = s_all.at[at_z(-step * (d if landed else d - 1)), h]
        return pltpu.make_async_remote_copy(
            src_ref=slot, dst_ref=slot,
            send_sem=z_send, recv_sem=z_recv.at[way, d - 1, h],
            device_id=(src_me, at_z(step)), device_id_type=MESH,
        )

    def piece(way, i):
        return (i + way * PIECES // 2) % PIECES

    def goes(d, i):
        return d < NZ // 2 or (d == NZ // 2 and i < PIECES // 2)

    def to_twin(dz, h):
        slot = s_all.at[at_z(dz), h]
        pltpu.make_async_remote_copy(
            src_ref=slot, dst_ref=slot, send_sem=d_send, recv_sem=d_recv.at[dz % NZ],
            device_id=twin, device_id_type=MESH,
        ).start()

    def from_twin(dz):
        slot = s_all.at[around(z, dz, NZ) * 2 + 1 - core]
        pltpu.make_async_remote_copy(
            src_ref=slot, dst_ref=slot, send_sem=d_send, recv_sem=d_recv.at[dz % NZ],
            device_id=twin, device_id_type=MESH,
        ).wait_recv()

    def z_event(d, i):
        for way in range(2):
            if goes(d, i):
                h = piece(way, i)
                z_copy(way, d, h, landed=True).wait_recv()
                if goes(d + 1, i):
                    z_copy(way, d + 1, h).start()
                to_twin(-d if way == 0 else d, h)

    def place(h, first, second):
        return at_xy(first, second) if h % 2 == 0 else at_xy(second, first)

    def p_copy(h, index, slice_at, move):
        slot = t_all.at[place(h, *slice_at), h]
        return pltpu.make_async_remote_copy(
            src_ref=slot, dst_ref=slot,
            send_sem=p_send, recv_sem=p_rest if index is None else p_recv.at[h, index],
            device_id=(place(h, *move), tgt_me), device_id_type=MESH,
        )

    up, down = (0, 1), (0, -1)
    offsets = (0, -1, 1, 2)
    upward = (True, False, False, False)

    def second(h, j):
        p_copy(h, 3 + j if upward[j] else None, (offsets[j], 0), up).start()
        p_copy(h, None if upward[j] else 3 + j, (offsets[j], 0), down).start()

    def below(h):
        p_copy(h, 0, (-1, 0), up).wait_recv()
        second(h, 1)

    def above(h):
        p_copy(h, 1, (1, 0), up).wait_recv()
        second(h, 2)

    def across(h):
        p_copy(h, 2, (2, 0), up).wait_recv()
        second(h, 3)

    def line(h, j):
        slice_at = (offsets[j], -1 if upward[j] else 1)
        p_copy(h, 3 + j, slice_at, up).wait_recv()
        p_copy(h, None, slice_at, up if upward[j] else down).start()

    for i in range(PIECES):
        for way in range(2):
            z_copy(way, 1, piece(way, i)).start()
    for h in range(QUARTERS):
        p_copy(h, 0, (0, 0), (1, 0)).start()
        p_copy(h, 1, (0, 0), (-1, 0)).start()
        p_copy(h, 2, (0, 0), (2, 0)).start()
    for h in range(QUARTERS):
        second(h, 0)
    for h in range(PIECES):
        to_twin(0, h)

    for b in range(row_blocks):
        scales = src_scale[:, b * LANES:(b + 1) * LANES]
        side[b * LANES:(b + 1) * LANES, :] = jnp.broadcast_to(scales, (LANES, LANES)).T
    columns[...] = jnp.full(columns.shape, LOW, F32)

    z_event(1, 0)
    for h in (0, 1):
        below(h)
        above(h)
    above(2)
    above(3)
    z_event(1, 1)
    across(0)
    z_event(1, 2)
    below(2)
    across(1)
    below(3)
    z_event(1, 3)
    line(0, 1)
    line(1, 1)
    z_event(2, 0)
    across(2)
    across(3)
    for h in (0, 1):
        line(h, 0)
    for h in (0, 1):
        line(h, 2)
    for h in (2, 3):
        line(h, 0)
    z_event(2, 1)
    for h in (2, 3):
        line(h, 2)
    line(0, 3)
    line(1, 3)
    z_event(2, 2)
    line(2, 1)
    line(3, 1)
    z_event(2, 3)
    line(2, 3)
    line(3, 3)
    for i in range(PIECES):
        z_event(3, i)
    pltpu.make_async_copy(t_all.at[pl.ds(0, 8)], t_all.at[pl.ds(0, 8)], p_rest).wait()

    def features(dz, part):
        return s_all[pl.ds(around(z, dz, NZ) * 2, 2), :, :, part].reshape(LANES, TILE)

    def targets(dz):
        return t_all[pl.ds(around(z, dz, NZ) * 2, 2)].reshape(LANES, sim.shape[1])

    def product(first, second, start, stop, fresh=False):
        @pl.loop(start, stop)
        def _(i):
            part = pl.ds(pl.multiple_of(i * TILE, TILE), TILE)
            left = jnp.concatenate([features(first, part), features(second, part)], axis=0)
            right = jnp.concatenate([targets(first), targets(second)], axis=0)
            dots = lax.dot_general(
                left, right, (((0,), (0,)), ((), ())), preferred_element_type=F32
            )
            if fresh:
                sim[part, :] = dots
            else:
                sim[part, :] = sim[part, :] + dots

    tiles = sim.shape[0] // TILE
    from_twin(-1)
    from_twin(1)
    product(-1, 1, 0, tiles, fresh=True)
    z_event(4, 0)
    from_twin(-2)
    from_twin(2)
    product(-2, 2, 0, tiles)
    z_event(4, 1)
    from_twin(-3)
    from_twin(3)
    product(-3, 3, 0, tiles)
    from_twin(0)
    from_twin(4)
    product(0, 4, 0, tiles)

    for slots, sem in ((s_all.at[pl.ds(0, 7)], z_send), (s_all.at[pl.ds(0, 8)], d_send),
                       (t_all.at[pl.ds(0, 15)], p_send)):
        pltpu.make_async_copy(slots, slots, sem).wait()

    def sweep(change):
        @pl.loop(0, row_blocks)
        def _(b):
            def rows(g):
                return pl.ds(pl.multiple_of(b * LANES + g * 8, 8), 8)

            for g in range(16):
                beside = side[rows(g), :]
                values = []
                for c in range(col_blocks):
                    lane = pl.ds(c * LANES, LANES)
                    value = change(sim[rows(g), lane], beside, c)
                    sim[rows(g), lane] = value
                    values.append(value)
                best = merge4(sort4(values[:4]), sort4(values[4:]))
                for k in range(4):
                    lists[k, g * 8:(g + 1) * 8, :] = best[k]
            turned = [lists[k].T for k in range(4)]
            best = over_sublanes(tree([[t[g * 8:(g + 1) * 8] for t in turned] for g in range(16)]))
            for k in range(4):
                row_out[pl.ds(row_line(k, b), 1), :] = best[k][0:1]
            for c in range(col_blocks):
                lane = pl.ds(c * LANES, LANES)
                quads = [
                    sort4([sim[rows(4 * q + g), lane] for g in range(4)]) for q in range(4)
                ]
                best = merge4(tree(quads), [columns[c, k] for k in range(4)])
                for k in range(4):
                    columns[c, k] = best[k]

        for c in range(col_blocks):
            best = over_sublanes([columns[c, k] for k in range(4)])
            for k in range(4):
                col_out[k, c:c + 1, :] = best[k][0:1]

    def exchange(stage):
        sends = []
        for r in range(1, NZ):
            sends.append(pltpu.make_async_remote_copy(
                src_ref=row_out, dst_ref=row_in.at[stage, r - 1],
                send_sem=x_send.at[0], recv_sem=x_recv.at[stage, 0],
                device_id=(src_me, at_z(r)), device_id_type=MESH,
            ))
        for r in range(1, GROUP):
            sends.append(pltpu.make_async_remote_copy(
                src_ref=col_out, dst_ref=col_in.at[stage, r - 1],
                send_sem=x_send.at[1], recv_sem=x_recv.at[stage, 1],
                device_id=(around(src_me, r, GROUP), tgt_me), device_id_type=MESH,
            ))
        for copy in sends:
            copy.start()
        row_slots, col_slots = row_in.at[stage], col_in.at[stage]

        pltpu.make_async_copy(row_slots, row_slots, x_recv.at[stage, 0]).wait()
        ours = [load_rows(row_out)] + [load_rows(row_in.at[stage, r]) for r in range(NZ - 1)]
        head, tail = tree([v[0] for v in ours]), tree([v[1] for v in ours])
        for k in range(4):
            pair_out[8 * k:8 * k + 8, :] = head[k]
            pair_out[TAIL[k]:TAIL[k] + 4, :] = tail[k][0:4]
        pair = pltpu.make_async_remote_copy(
            src_ref=pair_out, dst_ref=pair_in.at[stage],
            send_sem=x_send.at[2], recv_sem=x_recv.at[stage, 2],
            device_id=twin, device_id_type=MESH,
        )
        pair.start()

        pltpu.make_async_copy(col_slots, col_slots, x_recv.at[stage, 1]).wait()
        everyone = [[col_out[k] for k in range(4)]]
        everyone += [[col_in[stage, r, k] for k in range(4)] for r in range(GROUP - 1)]
        col_best = tree(everyone)

        pair.wait_recv()
        other_head, other_tail = load_rows(pair_in.at[stage])
        head, tail = merge4(head, other_head), merge4(tail, other_tail)
        pair.wait_send()
        pltpu.make_async_copy(row_slots, row_slots, x_send.at[0]).wait()
        pltpu.make_async_copy(col_slots, col_slots, x_send.at[1]).wait()
        return head, tail, col_best

    def line_of(head, tail, b):
        return head[b:b + 1] if b < 8 else tail[b - 8:b - 7]

    def scaled(value, beside, c):
        return value * beside * tgt_scale[:, c * LANES:(c + 1) * LANES]

    def half_mean(best):
        return (best[0] + best[1] + best[2] + best[3]) * 0.125

    sweep(scaled)
    head, tail, col_best = exchange(0)

    head, tail, beneath = half_mean(head), half_mean(tail), half_mean(col_best)
    for b in range(row_blocks):
        line = line_of(head, tail, b)
        side[b * LANES:(b + 1) * LANES, :] = jnp.broadcast_to(line, (LANES, LANES)).T
    for c in range(col_blocks):
        col_mean[c] = jnp.broadcast_to(beneath[c:c + 1], (8, LANES))
    columns[...] = jnp.full(columns.shape, LOW, F32)

    def margin(value, beside, c):
        return value / (beside + col_mean[c])

    sweep(margin)
    head, tail, col_best = exchange(1)
    for k in range(4):
        for b in range(row_blocks):
            fwd_ref[k:k + 1, b * LANES:(b + 1) * LANES] = line_of(head[k], tail[k], b)
        for c in range(col_blocks):
            bwd_ref[k:k + 1, c * LANES:(c + 1) * LANES] = col_best[k][c:c + 1]


def body(src_codes, src_scale, tgt_codes, tgt_scale):
    depth, rows = src_codes.shape
    cols = tgt_codes.shape[1]
    col_blocks = cols // LANES
    vmem = pl.BlockSpec(memory_space=pltpu.VMEM)
    hbm = pl.BlockSpec(memory_space=pltpu.HBM)
    dma = pltpu.SemaphoreType.DMA
    return pl.pallas_call(
        kernel,
        out_shape=(
            jax.ShapeDtypeStruct((4, rows), F32),
            jax.ShapeDtypeStruct((4, cols), F32),
        ),
        in_specs=[hbm, vmem, hbm, vmem],
        out_specs=(vmem, vmem),
        scratch_shapes=[
            pltpu.VMEM((GROUP, PIECES, depth // PIECES, rows), jnp.bfloat16),
            pltpu.VMEM((GROUP, QUARTERS, depth // QUARTERS, cols), jnp.bfloat16),
            pltpu.VMEM((rows, cols), F32),
            pltpu.VMEM((rows, LANES), F32),
            pltpu.VMEM((4, LANES, LANES), F32),
            pltpu.VMEM((col_blocks, 4, 8, LANES), F32),
            pltpu.VMEM((48, LANES), F32),
            pltpu.VMEM((2, NZ - 1, 48, LANES), F32),
            pltpu.VMEM((48, LANES), F32),
            pltpu.VMEM((2, 48, LANES), F32),
            pltpu.VMEM((4, 8, LANES), F32),
            pltpu.VMEM((2, GROUP - 1, 4, 8, LANES), F32),
            pltpu.VMEM((col_blocks, 8, LANES), F32),
            dma((2, 4)),
            dma,
            dma((2, NZ // 2, PIECES)),
            dma,
            dma((NZ,)),
            dma,
            dma((QUARTERS, 7)),
            dma,
            dma((3,)),
            dma((2, 3)),
        ],
        compiler_params=pltpu.CompilerParams(
            collective_id=0, has_side_effects=True, vmem_limit_bytes=55150 * 1024
        ),
        name="mine",
    )(src_codes, src_scale.reshape(1, rows), tgt_codes, tgt_scale.reshape(1, cols))


def solution(mesh):
    placed = (P("tgt", "src"), P("src"), P("src", "tgt"), P("tgt"))
    return jax.shard_map(
        body,
        mesh=mesh,
        in_specs=placed,
        out_specs=(P(None, "src"), P(None, "tgt")),
        check_vma=False,
    )
```

```python
import jax
import jax.numpy as jnp
from jax import lax
from jax.experimental import pallas as pl
from jax.experimental.pallas import tpu as pltpu
from jax.sharding import PartitionSpec as P

MESH = pl.DeviceIdType.MESH
F32 = jnp.float32
LOW = -1e30

NX, NY, NZ = 4, 4, 8
GROUP = 16
LANES = 128
PIECES = 4
QUARTERS = 4
TILE = 1536


def compare(a, b):
    return jnp.maximum(a, b), jnp.minimum(a, b)


def sort4(v):
    a, b = compare(v[0], v[1])
    c, d = compare(v[2], v[3])
    a, c = compare(a, c)
    b, d = compare(b, d)
    b, c = compare(b, c)
    return [a, b, c, d]


def merge4(p, q):
    a, b, c, d = [jnp.maximum(p[i], q[3 - i]) for i in range(4)]
    a, c = compare(a, c)
    b, d = compare(b, d)
    a, b = compare(a, b)
    c, d = compare(c, d)
    return [a, b, c, d]


def tree(lists):
    while len(lists) > 1:
        odd = lists[len(lists) // 2 * 2:]
        lists = [merge4(lists[i], lists[i + 1]) for i in range(0, len(lists) - 1, 2)] + odd
    return lists[0]


def over_sublanes(best):
    for shift in (4, 2, 1):
        best = merge4(best, [pltpu.roll(v, shift, 0) for v in best])
    return best


QUAD = (0, 8, 12, 4)


def load8(ref):
    return [ref[8 * k:8 * k + 8, :] for k in range(4)]


def load4(ref):
    first, second = ref[0:8, :], ref[8:16, :]
    return [first, second, pltpu.roll(second, 4, 0), pltpu.roll(first, 4, 0)]


def store8(ref, best):
    for k in range(4):
        ref[8 * k:8 * k + 8, :] = best[k]


def store4(ref, best):
    for k in range(4):
        ref[QUAD[k]:QUAD[k] + 4, :] = best[k][0:4]


HEAD, TAIL, LEFT, RIGHT = range(4)


def kernel(
    src_ref, src_scale, tgt_ref, tgt_scale, fwd_ref, bwd_ref,
    s_all, t_all, sim, side, lists, columns,
    head_out, head_in, head_pair, head_twin,
    tail_out, tail_in, tail_pair, tail_twin,
    left_out, left_in, right_out, right_in, col_mean,
    own_sem, z_send, z_recv, d_send, d_recv, p_send, p_recv, p_rest,
    x_send, x_recv,
):
    src_me, tgt_me = lax.axis_index("src"), lax.axis_index("tgt")
    x, y = src_me // NY, lax.rem(src_me, NY)
    z, core = tgt_me // 2, lax.rem(tgt_me, 2)
    row_blocks, col_blocks = sim.shape[0] // LANES, sim.shape[1] // LANES

    def around(v, step, n):
        return lax.rem(v + (step + n), n)

    def at_xy(dx, dy):
        return around(x, dx, NX) * NY + around(y, dy, NY)

    def at_z(dz):
        return around(z, dz, NZ) * 2 + core

    twin = (src_me, z * 2 + 1 - core)

    barrier = pltpu.get_barrier_semaphore()
    neighbours = [(src_me, at_z(1)), (src_me, at_z(-1)), twin]
    steps = ((1, 0), (-1, 0), (2, 0), (0, 1), (0, -1), (0, 2))
    neighbours += [(at_xy(*step), tgt_me) for step in steps]
    for device in neighbours:
        pl.semaphore_signal(barrier, inc=1, device_id=device, device_id_type=MESH)

    own = []
    for h in range(PIECES):
        part = pl.ds(h * 16, 16)
        own.append(pltpu.make_async_copy(src_ref.at[part], s_all.at[tgt_me, h], own_sem.at[0, h]))
    for h in range(QUARTERS):
        part = pl.ds(h * 16, 16)
        own.append(pltpu.make_async_copy(tgt_ref.at[part], t_all.at[src_me, h], own_sem.at[1, h]))
    for copy in own:
        copy.start()

    for copy in own:
        copy.wait()
    pl.semaphore_wait(barrier, len(neighbours))

    def z_copy(way, d, h, landed=False):
        step = 1 if way == 0 else -1
        slot = s_all.at[at_z(-step * (d if landed else d - 1)), h]
        return pltpu.make_async_remote_copy(
            src_ref=slot, dst_ref=slot,
            send_sem=z_send, recv_sem=z_recv.at[way, d - 1, h],
            device_id=(src_me, at_z(step)), device_id_type=MESH,
        )

    def piece(way, i):
        return (i + way * PIECES // 2) % PIECES

    def goes(d, i):
        return d < NZ // 2 or (d == NZ // 2 and i < PIECES // 2)

    def to_twin(dz, h):
        slot = s_all.at[at_z(dz), h]
        pltpu.make_async_remote_copy(
            src_ref=slot, dst_ref=slot, send_sem=d_send, recv_sem=d_recv.at[dz % NZ],
            device_id=twin, device_id_type=MESH,
        ).start()

    def from_twin(dz):
        slot = s_all.at[around(z, dz, NZ) * 2 + 1 - core]
        pltpu.make_async_remote_copy(
            src_ref=slot, dst_ref=slot, send_sem=d_send, recv_sem=d_recv.at[dz % NZ],
            device_id=twin, device_id_type=MESH,
        ).wait_recv()

    def z_event(d, i):
        for way in range(2):
            if goes(d, i):
                h = piece(way, i)
                z_copy(way, d, h, landed=True).wait_recv()
                if goes(d + 1, i):
                    z_copy(way, d + 1, h).start()
                to_twin(-d if way == 0 else d, h)

    def place(h, first, second):
        return at_xy(first, second) if h % 2 == 0 else at_xy(second, first)

    def p_copy(h, index, slice_at, move):
        slot = t_all.at[place(h, *slice_at), h]
        return pltpu.make_async_remote_copy(
            src_ref=slot, dst_ref=slot,
            send_sem=p_send, recv_sem=p_rest if index is None else p_recv.at[h, index],
            device_id=(place(h, *move), tgt_me), device_id_type=MESH,
        )

    up, down = (0, 1), (0, -1)
    offsets = (0, -1, 1, 2)
    upward = (True, False, False, False)

    def second(h, j):
        p_copy(h, 3 + j if upward[j] else None, (offsets[j], 0), up).start()
        p_copy(h, None if upward[j] else 3 + j, (offsets[j], 0), down).start()

    def below(h):
        p_copy(h, 0, (-1, 0), up).wait_recv()
        second(h, 1)

    def above(h):
        p_copy(h, 1, (1, 0), up).wait_recv()
        second(h, 2)

    def across(h):
        p_copy(h, 2, (2, 0), up).wait_recv()
        second(h, 3)

    def line(h, j):
        slice_at = (offsets[j], -1 if upward[j] else 1)
        p_copy(h, 3 + j, slice_at, up).wait_recv()
        p_copy(h, None, slice_at, up if upward[j] else down).start()

    for i in range(PIECES):
        for way in range(2):
            z_copy(way, 1, piece(way, i)).start()
    for h in range(QUARTERS):
        p_copy(h, 0, (0, 0), (1, 0)).start()
        p_copy(h, 1, (0, 0), (-1, 0)).start()
        p_copy(h, 2, (0, 0), (2, 0)).start()
    for h in range(QUARTERS):
        second(h, 0)
    for h in range(PIECES):
        to_twin(0, h)

    for b in range(row_blocks):
        scales = src_scale[:, b * LANES:(b + 1) * LANES]
        side[b * LANES:(b + 1) * LANES, :] = jnp.broadcast_to(scales, (LANES, LANES)).T
    columns[...] = jnp.full(columns.shape, LOW, F32)

    z_event(1, 0)
    for h in (0, 1):
        below(h)
        above(h)
    above(2)
    above(3)
    z_event(1, 1)
    across(0)
    z_event(1, 2)
    below(2)
    across(1)
    below(3)
    z_event(1, 3)
    line(0, 1)
    line(1, 1)
    z_event(2, 0)
    across(2)
    across(3)
    for h in (0, 1):
        line(h, 0)
    for h in (0, 1):
        line(h, 2)
    for h in (2, 3):
        line(h, 0)
    z_event(2, 1)
    for h in (2, 3):
        line(h, 2)
    line(0, 3)
    line(1, 3)
    z_event(2, 2)
    line(2, 1)
    line(3, 1)
    z_event(2, 3)
    line(2, 3)
    line(3, 3)
    for i in range(PIECES):
        z_event(3, i)
    pltpu.make_async_copy(t_all.at[pl.ds(0, 8)], t_all.at[pl.ds(0, 8)], p_rest).wait()

    def features(dz, part):
        return s_all[pl.ds(around(z, dz, NZ) * 2, 2), :, :, part].reshape(LANES, TILE)

    def targets(dz):
        return t_all[pl.ds(around(z, dz, NZ) * 2, 2)].reshape(LANES, sim.shape[1])

    def product(first, second, start, stop, fresh=False):
        @pl.loop(start, stop)
        def _(i):
            part = pl.ds(pl.multiple_of(i * TILE, TILE), TILE)
            left = jnp.concatenate([features(first, part), features(second, part)], axis=0)
            right = jnp.concatenate([targets(first), targets(second)], axis=0)
            dots = lax.dot_general(
                left, right, (((0,), (0,)), ((), ())), preferred_element_type=F32
            )
            if fresh:
                sim[part, :] = dots
            else:
                sim[part, :] = sim[part, :] + dots

    tiles = sim.shape[0] // TILE
    from_twin(-1)
    from_twin(1)
    product(-1, 1, 0, tiles, fresh=True)
    z_event(4, 0)
    from_twin(-2)
    from_twin(2)
    product(-2, 2, 0, tiles)
    z_event(4, 1)
    from_twin(-3)
    from_twin(3)
    product(-3, 3, 0, tiles)
    from_twin(0)
    from_twin(4)
    product(0, 4, 0, tiles)

    for slots, sem in ((s_all.at[pl.ds(0, 7)], z_send), (s_all.at[pl.ds(0, 8)], d_send),
                       (t_all.at[pl.ds(0, 15)], p_send)):
        pltpu.make_async_copy(slots, slots, sem).wait()

    out = (head_out, tail_out, left_out, right_out)
    into = (head_in, tail_in, left_in, right_in)

    def sweep(stage, change):
        def best_of_rows(b):
            def rows(g):
                return pl.ds(pl.multiple_of(b * LANES + g * 8, 8), 8)

            for g in range(16):
                beside = side[rows(g), :]
                values = []
                for c in range(col_blocks):
                    lane = pl.ds(c * LANES, LANES)
                    value = change(sim[rows(g), lane], beside, c)
                    sim[rows(g), lane] = value
                    values.append(value)
                best = merge4(sort4(values[:4]), sort4(values[4:]))
                for k in range(4):
                    lists[k, g * 8:(g + 1) * 8, :] = best[k]
            turned = [lists[k].T for k in range(4)]
            return over_sublanes(tree([[t[g * 8:(g + 1) * 8] for t in turned] for g in range(16)]))

        @pl.loop(0, 8)
        def _(b):
            best = best_of_rows(b)
            for k in range(4):
                head_out[pl.ds(8 * k + b, 1), :] = best[k][0:1]

        send(stage, HEAD)

        @pl.loop(8, row_blocks)
        def _(b):
            best = best_of_rows(b)
            for k in range(4):
                tail_out[pl.ds(QUAD[k] + b - 8, 1), :] = best[k][0:1]

        send(stage, TAIL)

        for part in (LEFT, RIGHT):
            first = 0 if part == LEFT else 4

            @pl.loop(0, row_blocks)
            def _(b, first=first):
                for c in range(first, first + 4):
                    lane = pl.ds(c * LANES, LANES)
                    quads = [
                        sort4([
                            sim[pl.ds(pl.multiple_of(b * LANES + (4 * q + g) * 8, 8), 8), lane]
                            for g in range(4)
                        ])
                        for q in range(4)
                    ]
                    best = merge4(tree(quads), [columns[c, k] for k in range(4)])
                    for k in range(4):
                        columns[c, k] = best[k]

            for c in range(4):
                best = over_sublanes([columns[first + c, k] for k in range(4)])
                for k in range(4):
                    out[part][QUAD[k] + c:QUAD[k] + c + 1, :] = best[k][0:1]
            send(stage, part)

    def send(stage, part):
        for r in range(1, NZ if part in (HEAD, TAIL) else GROUP):
            device = (
                (src_me, at_z(r)) if part in (HEAD, TAIL) else (around(src_me, r, GROUP), tgt_me)
            )
            pltpu.make_async_remote_copy(
                src_ref=out[part], dst_ref=into[part].at[stage, r - 1],
                send_sem=x_send.at[part], recv_sem=x_recv.at[stage, part],
                device_id=device, device_id_type=MESH,
            ).start()

    def gathered(stage, part):
        slots = into[part].at[stage]
        pltpu.make_async_copy(slots, slots, x_recv.at[stage, part]).wait()
        load = load8 if part == HEAD else load4
        count = into[part].shape[1]
        best = tree([load(out[part])] + [load(into[part].at[stage, r]) for r in range(count)])
        return best

    def sent(stage):
        for part in (HEAD, TAIL, LEFT, RIGHT):
            slots = into[part].at[stage]
            pltpu.make_async_copy(slots, slots, x_send.at[part]).wait()

    def twin_copy(stage, part):
        mine, theirs = ((head_pair, head_twin), (tail_pair, tail_twin))[part]
        return pltpu.make_async_remote_copy(
            src_ref=mine, dst_ref=theirs.at[stage],
            send_sem=x_send.at[4 + part], recv_sem=x_recv.at[stage, 4 + part],
            device_id=twin, device_id_type=MESH,
        )

    def combined(stage, use_head, use_tail, use_cols):
        head = gathered(stage, HEAD)
        store8(head_pair, head)
        twin_copy(stage, HEAD).start()
        tail = gathered(stage, TAIL)
        store4(tail_pair, tail)
        twin_copy(stage, TAIL).start()
        use_cols(0, gathered(stage, LEFT))
        twin_copy(stage, HEAD).wait_recv()
        use_head(merge4(head, load8(head_twin.at[stage])))
        twin_copy(stage, TAIL).wait_recv()
        use_tail(merge4(tail, load4(tail_twin.at[stage])))
        use_cols(4, gathered(stage, RIGHT))
        for part in (HEAD, TAIL):
            twin_copy(stage, part).wait_send()
        sent(stage)

    def scaled(value, beside, c):
        return value * beside * tgt_scale[:, c * LANES:(c + 1) * LANES]

    def half_mean(best):
        return (best[0] + best[1] + best[2] + best[3]) * 0.125

    def rows_mean(first, count):
        def use(best):
            mean = half_mean(best)
            for b in range(count):
                at = (first + b) * LANES
                side[at:at + LANES, :] = jnp.broadcast_to(mean[b:b + 1], (LANES, LANES)).T
        return use

    def cols_mean(first, best):
        mean = half_mean(best)
        for c in range(4):
            col_mean[first + c] = jnp.broadcast_to(mean[c:c + 1], (8, LANES))

    sweep(0, scaled)
    combined(0, rows_mean(0, 8), rows_mean(8, row_blocks - 8), cols_mean)

    columns[...] = jnp.full(columns.shape, LOW, F32)

    def margin(value, beside, c):
        return value / (beside + col_mean[c])

    def rows_out(first, count):
        def use(best):
            for k in range(4):
                for b in range(count):
                    at = (first + b) * LANES
                    fwd_ref[k:k + 1, at:at + LANES] = best[k][b:b + 1]
        return use

    def cols_out(first, best):
        for k in range(4):
            for c in range(4):
                at = (first + c) * LANES
                bwd_ref[k:k + 1, at:at + LANES] = best[k][c:c + 1]

    sweep(1, margin)
    combined(1, rows_out(0, 8), rows_out(8, row_blocks - 8), cols_out)


def body(src_codes, src_scale, tgt_codes, tgt_scale):
    depth, rows = src_codes.shape
    cols = tgt_codes.shape[1]
    col_blocks = cols // LANES
    vmem = pl.BlockSpec(memory_space=pltpu.VMEM)
    hbm = pl.BlockSpec(memory_space=pltpu.HBM)
    dma = pltpu.SemaphoreType.DMA
    return pl.pallas_call(
        kernel,
        out_shape=(
            jax.ShapeDtypeStruct((4, rows), F32),
            jax.ShapeDtypeStruct((4, cols), F32),
        ),
        in_specs=[hbm, vmem, hbm, vmem],
        out_specs=(vmem, vmem),
        scratch_shapes=[
            pltpu.VMEM((GROUP, PIECES, depth // PIECES, rows), jnp.bfloat16),
            pltpu.VMEM((GROUP, QUARTERS, depth // QUARTERS, cols), jnp.bfloat16),
            pltpu.VMEM((rows, cols), F32),
            pltpu.VMEM((rows, LANES), F32),
            pltpu.VMEM((4, LANES, LANES), F32),
            pltpu.VMEM((col_blocks, 4, 8, LANES), F32),
            pltpu.VMEM((32, LANES), F32),
            pltpu.VMEM((2, NZ - 1, 32, LANES), F32),
            pltpu.VMEM((32, LANES), F32),
            pltpu.VMEM((2, 32, LANES), F32),
            pltpu.VMEM((16, LANES), F32),
            pltpu.VMEM((2, NZ - 1, 16, LANES), F32),
            pltpu.VMEM((16, LANES), F32),
            pltpu.VMEM((2, 16, LANES), F32),
            pltpu.VMEM((16, LANES), F32),
            pltpu.VMEM((2, GROUP - 1, 16, LANES), F32),
            pltpu.VMEM((16, LANES), F32),
            pltpu.VMEM((2, GROUP - 1, 16, LANES), F32),
            pltpu.VMEM((col_blocks, 8, LANES), F32),
            dma((2, 4)),
            dma,
            dma((2, NZ // 2, PIECES)),
            dma,
            dma((NZ,)),
            dma,
            dma((QUARTERS, 7)),
            dma,
            dma((6,)),
            dma((2, 6)),
        ],
        compiler_params=pltpu.CompilerParams(
            collective_id=0, has_side_effects=True, vmem_limit_bytes=55150 * 1024
        ),
        name="mine",
    )(src_codes, src_scale.reshape(1, rows), tgt_codes, tgt_scale.reshape(1, cols))


def solution(mesh):
    placed = (P("tgt", "src"), P("src"), P("src", "tgt"), P("tgt"))
    return jax.shard_map(
        body,
        mesh=mesh,
        in_specs=placed,
        out_specs=(P(None, "src"), P(None, "tgt")),
        check_vma=False,
    )
```

```python
import jax
import jax.numpy as jnp
from jax import lax
from jax.experimental import pallas as pl
from jax.experimental.pallas import tpu as pltpu
from jax.sharding import PartitionSpec as P

MESH = pl.DeviceIdType.MESH
F32 = jnp.float32
LOW = -1e30

NX, NY, NZ = 4, 4, 8
GROUP = 16
LANES = 128
PIECES = 4
QUARTERS = 4
TILE = 1536


def compare(a, b):
    return jnp.maximum(a, b), jnp.minimum(a, b)


def sort4(v):
    a, b = compare(v[0], v[1])
    c, d = compare(v[2], v[3])
    a, c = compare(a, c)
    b, d = compare(b, d)
    b, c = compare(b, c)
    return [a, b, c, d]


def merge4(p, q):
    a, b, c, d = [jnp.maximum(p[i], q[3 - i]) for i in range(4)]
    a, c = compare(a, c)
    b, d = compare(b, d)
    a, b = compare(a, b)
    c, d = compare(c, d)
    return [a, b, c, d]


def tree(lists):
    while len(lists) > 1:
        odd = lists[len(lists) // 2 * 2:]
        lists = [merge4(lists[i], lists[i + 1]) for i in range(0, len(lists) - 1, 2)] + odd
    return lists[0]


def over_sublanes(best):
    for shift in (4, 2, 1):
        best = merge4(best, [pltpu.roll(v, shift, 0) for v in best])
    return best


QUAD = (0, 8, 12, 4)


def load8(ref):
    return [ref[8 * k:8 * k + 8, :] for k in range(4)]


def load4(ref):
    first, second = ref[0:8, :], ref[8:16, :]
    return [first, second, pltpu.roll(second, 4, 0), pltpu.roll(first, 4, 0)]


def store8(ref, best):
    for k in range(4):
        ref[8 * k:8 * k + 8, :] = best[k]


def store4(ref, best):
    for k in range(4):
        ref[QUAD[k]:QUAD[k] + 4, :] = best[k][0:4]


HEAD, TAIL, LEFT, RIGHT = range(4)


def kernel(
    src_ref, src_scale, tgt_ref, tgt_scale, fwd_ref, bwd_ref,
    s_all, t_all, sim, side, lists, columns,
    head_out, head_in, head_pair, head_twin,
    tail_out, tail_in, tail_pair, tail_twin,
    left_out, left_in, right_out, right_in, col_mean,
    own_sem, z_send, z_recv, d_send, d_recv, p_send, p_recv, p_rest,
    x_send, x_recv,
):
    src_me, tgt_me = lax.axis_index("src"), lax.axis_index("tgt")
    x, y = src_me // NY, lax.rem(src_me, NY)
    z, core = tgt_me // 2, lax.rem(tgt_me, 2)
    row_blocks, col_blocks = sim.shape[0] // LANES, sim.shape[1] // LANES

    def around(v, step, n):
        return lax.rem(v + (step + n), n)

    def at_xy(dx, dy):
        return around(x, dx, NX) * NY + around(y, dy, NY)

    def at_z(dz):
        return around(z, dz, NZ) * 2 + core

    twin = (src_me, z * 2 + 1 - core)

    barrier = pltpu.get_barrier_semaphore()
    neighbours = [(src_me, at_z(1)), (src_me, at_z(-1)), twin]
    steps = ((1, 0), (-1, 0), (2, 0), (0, 1), (0, -1), (0, 2))
    neighbours += [(at_xy(*step), tgt_me) for step in steps]
    for device in neighbours:
        pl.semaphore_signal(barrier, inc=1, device_id=device, device_id_type=MESH)

    own = []
    for h in range(PIECES):
        part = pl.ds(h * 16, 16)
        own.append(pltpu.make_async_copy(src_ref.at[part], s_all.at[tgt_me, h], own_sem.at[0, h]))
    for h in range(QUARTERS):
        part = pl.ds(h * 16, 16)
        own.append(pltpu.make_async_copy(tgt_ref.at[part], t_all.at[src_me, h], own_sem.at[1, h]))
    for copy in own:
        copy.start()

    for copy in own:
        copy.wait()
    pl.semaphore_wait(barrier, len(neighbours))

    def z_copy(way, d, h, landed=False):
        step = 1 if way == 0 else -1
        slot = s_all.at[at_z(-step * (d if landed else d - 1)), h]
        return pltpu.make_async_remote_copy(
            src_ref=slot, dst_ref=slot,
            send_sem=z_send, recv_sem=z_recv.at[way, d - 1, h],
            device_id=(src_me, at_z(step)), device_id_type=MESH,
        )

    def piece(way, i):
        return (i + way * PIECES // 2) % PIECES

    def goes(d, i):
        return d < NZ // 2 or (d == NZ // 2 and i < PIECES // 2)

    def to_twin(dz, h):
        slot = s_all.at[at_z(dz), h]
        pltpu.make_async_remote_copy(
            src_ref=slot, dst_ref=slot, send_sem=d_send, recv_sem=d_recv.at[dz % NZ],
            device_id=twin, device_id_type=MESH,
        ).start()

    def from_twin(dz):
        slot = s_all.at[around(z, dz, NZ) * 2 + 1 - core]
        pltpu.make_async_remote_copy(
            src_ref=slot, dst_ref=slot, send_sem=d_send, recv_sem=d_recv.at[dz % NZ],
            device_id=twin, device_id_type=MESH,
        ).wait_recv()

    def z_event(d, i):
        for way in range(2):
            if goes(d, i):
                h = piece(way, i)
                z_copy(way, d, h, landed=True).wait_recv()
                if goes(d + 1, i):
                    z_copy(way, d + 1, h).start()
                to_twin(-d if way == 0 else d, h)

    def place(h, first, second):
        return at_xy(first, second) if h % 2 == 0 else at_xy(second, first)

    def p_copy(h, index, slice_at, move):
        slot = t_all.at[place(h, *slice_at), h]
        return pltpu.make_async_remote_copy(
            src_ref=slot, dst_ref=slot,
            send_sem=p_send, recv_sem=p_rest if index is None else p_recv.at[h, index],
            device_id=(place(h, *move), tgt_me), device_id_type=MESH,
        )

    up, down = (0, 1), (0, -1)
    offsets = (0, -1, 1, 2)
    upward = (True, False, False, False)

    def second(h, j):
        p_copy(h, 3 + j if upward[j] else None, (offsets[j], 0), up).start()
        p_copy(h, None if upward[j] else 3 + j, (offsets[j], 0), down).start()

    def below(h):
        p_copy(h, 0, (-1, 0), up).wait_recv()
        second(h, 1)

    def above(h):
        p_copy(h, 1, (1, 0), up).wait_recv()
        second(h, 2)

    def across(h):
        p_copy(h, 2, (2, 0), up).wait_recv()
        second(h, 3)

    def line(h, j):
        slice_at = (offsets[j], -1 if upward[j] else 1)
        p_copy(h, 3 + j, slice_at, up).wait_recv()
        p_copy(h, None, slice_at, up if upward[j] else down).start()

    for i in range(PIECES):
        for way in range(2):
            z_copy(way, 1, piece(way, i)).start()
    for h in range(QUARTERS):
        p_copy(h, 0, (0, 0), (1, 0)).start()
        p_copy(h, 1, (0, 0), (-1, 0)).start()
        p_copy(h, 2, (0, 0), (2, 0)).start()
    for h in range(QUARTERS):
        second(h, 0)
    for h in range(PIECES):
        to_twin(0, h)

    for b in range(row_blocks):
        scales = src_scale[:, b * LANES:(b + 1) * LANES]
        side[b * LANES:(b + 1) * LANES, :] = jnp.broadcast_to(scales, (LANES, LANES)).T
    columns[...] = jnp.full(columns.shape, LOW, F32)

    z_event(1, 0)
    for h in (0, 1):
        below(h)
        above(h)
    above(2)
    above(3)
    z_event(1, 1)
    across(0)
    z_event(1, 2)
    below(2)
    across(1)
    below(3)
    z_event(1, 3)
    line(0, 1)
    line(1, 1)
    z_event(2, 0)
    across(2)
    across(3)
    for h in (0, 1):
        line(h, 0)
    for h in (0, 1):
        line(h, 2)
    for h in (2, 3):
        line(h, 0)
    z_event(2, 1)
    for h in (2, 3):
        line(h, 2)
    line(0, 3)
    line(1, 3)
    z_event(2, 2)
    line(2, 1)
    line(3, 1)
    z_event(2, 3)
    line(2, 3)
    line(3, 3)
    for i in range(PIECES):
        z_event(3, i)
    pltpu.make_async_copy(t_all.at[pl.ds(0, 8)], t_all.at[pl.ds(0, 8)], p_rest).wait()

    def features(dz, part):
        return s_all[pl.ds(around(z, dz, NZ) * 2, 2), :, :, part].reshape(LANES, TILE)

    def targets(dz):
        return t_all[pl.ds(around(z, dz, NZ) * 2, 2)].reshape(LANES, sim.shape[1])

    def product(first, second, start, stop, fresh=False):
        @pl.loop(start, stop)
        def _(i):
            part = pl.ds(pl.multiple_of(i * TILE, TILE), TILE)
            left = jnp.concatenate([features(first, part), features(second, part)], axis=0)
            right = jnp.concatenate([targets(first), targets(second)], axis=0)
            dots = lax.dot_general(
                left, right, (((0,), (0,)), ((), ())), preferred_element_type=F32
            )
            if fresh:
                sim[part, :] = dots
            else:
                sim[part, :] = sim[part, :] + dots

    tiles = sim.shape[0] // TILE
    from_twin(-1)
    from_twin(1)
    product(-1, 1, 0, tiles, fresh=True)
    z_event(4, 0)
    from_twin(-2)
    from_twin(2)
    product(-2, 2, 0, tiles)
    z_event(4, 1)
    from_twin(-3)
    from_twin(3)
    product(-3, 3, 0, tiles)
    from_twin(0)
    from_twin(4)
    product(0, 4, 0, tiles)

    for slots, sem in ((s_all.at[pl.ds(0, 7)], z_send), (s_all.at[pl.ds(0, 8)], d_send),
                       (t_all.at[pl.ds(0, 15)], p_send)):
        pltpu.make_async_copy(slots, slots, sem).wait()

    out = (head_out, tail_out, left_out, right_out)
    into = (head_in, tail_in, left_in, right_in)

    def sweep(stage, change):
        def best_of_rows(b):
            def rows(g):
                return pl.ds(pl.multiple_of(b * LANES + g * 8, 8), 8)

            for g in range(16):
                beside = side[rows(g), :]
                values = []
                for c in range(col_blocks):
                    lane = pl.ds(c * LANES, LANES)
                    value = change(sim[rows(g), lane], beside, c)
                    sim[rows(g), lane] = value
                    values.append(value)
                best = merge4(sort4(values[:4]), sort4(values[4:]))
                for k in range(4):
                    lists[k, g * 8:(g + 1) * 8, :] = best[k]
            turned = [lists[k].T for k in range(4)]
            return over_sublanes(tree([[t[g * 8:(g + 1) * 8] for t in turned] for g in range(16)]))

        @pl.loop(0, 8, unroll=4)
        def _(b):
            best = best_of_rows(b)
            for k in range(4):
                head_out[pl.ds(8 * k + b, 1), :] = best[k][0:1]

        send(stage, HEAD)

        @pl.loop(8, row_blocks, unroll=4)
        def _(b):
            best = best_of_rows(b)
            for k in range(4):
                tail_out[pl.ds(QUAD[k] + b - 8, 1), :] = best[k][0:1]

        send(stage, TAIL)

        for part in (LEFT, RIGHT):
            first = 0 if part == LEFT else 4

            @pl.loop(0, row_blocks)
            def _(b, first=first):
                for c in range(first, first + 4):
                    lane = pl.ds(c * LANES, LANES)
                    quads = [
                        sort4([
                            sim[pl.ds(pl.multiple_of(b * LANES + (4 * q + g) * 8, 8), 8), lane]
                            for g in range(4)
                        ])
                        for q in range(4)
                    ]
                    best = merge4(tree(quads), [columns[c, k] for k in range(4)])
                    for k in range(4):
                        columns[c, k] = best[k]

            for c in range(4):
                best = over_sublanes([columns[first + c, k] for k in range(4)])
                for k in range(4):
                    out[part][QUAD[k] + c:QUAD[k] + c + 1, :] = best[k][0:1]
            send(stage, part)

    def send(stage, part):
        for r in range(1, NZ if part in (HEAD, TAIL) else GROUP):
            device = (
                (src_me, at_z(r)) if part in (HEAD, TAIL) else (around(src_me, r, GROUP), tgt_me)
            )
            pltpu.make_async_remote_copy(
                src_ref=out[part], dst_ref=into[part].at[stage, r - 1],
                send_sem=x_send.at[part], recv_sem=x_recv.at[stage, part],
                device_id=device, device_id_type=MESH,
            ).start()

    def gathered(stage, part):
        slots = into[part].at[stage]
        pltpu.make_async_copy(slots, slots, x_recv.at[stage, part]).wait()
        load = load8 if part == HEAD else load4
        count = into[part].shape[1]
        best = tree([load(out[part])] + [load(into[part].at[stage, r]) for r in range(count)])
        return best

    def sent(stage):
        for part in (HEAD, TAIL, LEFT, RIGHT):
            slots = into[part].at[stage]
            pltpu.make_async_copy(slots, slots, x_send.at[part]).wait()

    def twin_copy(stage, part):
        mine, theirs = ((head_pair, head_twin), (tail_pair, tail_twin))[part]
        return pltpu.make_async_remote_copy(
            src_ref=mine, dst_ref=theirs.at[stage],
            send_sem=x_send.at[4 + part], recv_sem=x_recv.at[stage, 4 + part],
            device_id=twin, device_id_type=MESH,
        )

    def combined(stage, use_head, use_tail, use_cols):
        head = gathered(stage, HEAD)
        store8(head_pair, head)
        twin_copy(stage, HEAD).start()
        tail = gathered(stage, TAIL)
        store4(tail_pair, tail)
        twin_copy(stage, TAIL).start()
        use_cols(0, gathered(stage, LEFT))
        twin_copy(stage, HEAD).wait_recv()
        use_head(merge4(head, load8(head_twin.at[stage])))
        twin_copy(stage, TAIL).wait_recv()
        use_tail(merge4(tail, load4(tail_twin.at[stage])))
        use_cols(4, gathered(stage, RIGHT))
        for part in (HEAD, TAIL):
            twin_copy(stage, part).wait_send()
        sent(stage)

    def scaled(value, beside, c):
        return value * beside * tgt_scale[:, c * LANES:(c + 1) * LANES]

    def half_mean(best):
        return (best[0] + best[1] + best[2] + best[3]) * 0.125

    def rows_mean(first, count):
        def use(best):
            mean = half_mean(best)
            for b in range(count):
                at = (first + b) * LANES
                side[at:at + LANES, :] = jnp.broadcast_to(mean[b:b + 1], (LANES, LANES)).T
        return use

    def cols_mean(first, best):
        mean = half_mean(best)
        for c in range(4):
            col_mean[first + c] = jnp.broadcast_to(mean[c:c + 1], (8, LANES))

    sweep(0, scaled)
    combined(0, rows_mean(0, 8), rows_mean(8, row_blocks - 8), cols_mean)

    columns[...] = jnp.full(columns.shape, LOW, F32)

    def margin(value, beside, c):
        return value / (beside + col_mean[c])

    def rows_out(first, count):
        def use(best):
            for k in range(4):
                for b in range(count):
                    at = (first + b) * LANES
                    fwd_ref[k:k + 1, at:at + LANES] = best[k][b:b + 1]
        return use

    def cols_out(first, best):
        for k in range(4):
            for c in range(4):
                at = (first + c) * LANES
                bwd_ref[k:k + 1, at:at + LANES] = best[k][c:c + 1]

    sweep(1, margin)
    combined(1, rows_out(0, 8), rows_out(8, row_blocks - 8), cols_out)


def body(src_codes, src_scale, tgt_codes, tgt_scale):
    depth, rows = src_codes.shape
    cols = tgt_codes.shape[1]
    col_blocks = cols // LANES
    vmem = pl.BlockSpec(memory_space=pltpu.VMEM)
    hbm = pl.BlockSpec(memory_space=pltpu.HBM)
    dma = pltpu.SemaphoreType.DMA
    return pl.pallas_call(
        kernel,
        out_shape=(
            jax.ShapeDtypeStruct((4, rows), F32),
            jax.ShapeDtypeStruct((4, cols), F32),
        ),
        in_specs=[hbm, vmem, hbm, vmem],
        out_specs=(vmem, vmem),
        scratch_shapes=[
            pltpu.VMEM((GROUP, PIECES, depth // PIECES, rows), jnp.bfloat16),
            pltpu.VMEM((GROUP, QUARTERS, depth // QUARTERS, cols), jnp.bfloat16),
            pltpu.VMEM((rows, cols), F32),
            pltpu.VMEM((rows, LANES), F32),
            pltpu.VMEM((4, LANES, LANES), F32),
            pltpu.VMEM((col_blocks, 4, 8, LANES), F32),
            pltpu.VMEM((32, LANES), F32),
            pltpu.VMEM((2, NZ - 1, 32, LANES), F32),
            pltpu.VMEM((32, LANES), F32),
            pltpu.VMEM((2, 32, LANES), F32),
            pltpu.VMEM((16, LANES), F32),
            pltpu.VMEM((2, NZ - 1, 16, LANES), F32),
            pltpu.VMEM((16, LANES), F32),
            pltpu.VMEM((2, 16, LANES), F32),
            pltpu.VMEM((16, LANES), F32),
            pltpu.VMEM((2, GROUP - 1, 16, LANES), F32),
            pltpu.VMEM((16, LANES), F32),
            pltpu.VMEM((2, GROUP - 1, 16, LANES), F32),
            pltpu.VMEM((col_blocks, 8, LANES), F32),
            dma((2, 4)),
            dma,
            dma((2, NZ // 2, PIECES)),
            dma,
            dma((NZ,)),
            dma,
            dma((QUARTERS, 7)),
            dma,
            dma((6,)),
            dma((2, 6)),
        ],
        compiler_params=pltpu.CompilerParams(
            collective_id=0, has_side_effects=True, vmem_limit_bytes=55150 * 1024
        ),
        name="mine",
    )(src_codes, src_scale.reshape(1, rows), tgt_codes, tgt_scale.reshape(1, cols))


def solution(mesh):
    placed = (P("tgt", "src"), P("src"), P("src", "tgt"), P("tgt"))
    return jax.shard_map(
        body,
        mesh=mesh,
        in_specs=placed,
        out_specs=(P(None, "src"), P(None, "tgt")),
        check_vma=False,
    )
```

```python
import jax
import jax.numpy as jnp
from jax import lax
from jax.experimental import pallas as pl
from jax.experimental.pallas import tpu as pltpu
from jax.sharding import PartitionSpec as P

MESH = pl.DeviceIdType.MESH
F32 = jnp.float32
LOW = -1e30

NX, NY, NZ = 4, 4, 8
GROUP = 16
LANES = 128
PIECES = 4
QUARTERS = 4
TILE = 1536


def compare(a, b):
    return jnp.maximum(a, b), jnp.minimum(a, b)


def sort4(v):
    a, b = compare(v[0], v[1])
    c, d = compare(v[2], v[3])
    a, c = compare(a, c)
    b, d = compare(b, d)
    b, c = compare(b, c)
    return [a, b, c, d]


def merge4(p, q):
    a, b, c, d = [jnp.maximum(p[i], q[3 - i]) for i in range(4)]
    a, c = compare(a, c)
    b, d = compare(b, d)
    a, b = compare(a, b)
    c, d = compare(c, d)
    return [a, b, c, d]


def tree(lists):
    while len(lists) > 1:
        odd = lists[len(lists) // 2 * 2:]
        lists = [merge4(lists[i], lists[i + 1]) for i in range(0, len(lists) - 1, 2)] + odd
    return lists[0]


def over_sublanes(best):
    for shift in (4, 2, 1):
        best = merge4(best, [pltpu.roll(v, shift, 0) for v in best])
    return best


QUAD = (0, 8, 12, 4)


def load8(ref):
    return [ref[8 * k:8 * k + 8, :] for k in range(4)]


def load4(ref):
    first, second = ref[0:8, :], ref[8:16, :]
    return [first, second, pltpu.roll(second, 4, 0), pltpu.roll(first, 4, 0)]


def store8(ref, best):
    for k in range(4):
        ref[8 * k:8 * k + 8, :] = best[k]


def store4(ref, best):
    for k in range(4):
        ref[QUAD[k]:QUAD[k] + 4, :] = best[k][0:4]


HEAD, TAIL, LEFT, RIGHT = range(4)


def kernel(
    src_ref, src_scale, tgt_ref, tgt_scale, fwd_ref, bwd_ref,
    s_all, t_all, sim, side, lists, columns,
    head_out, head_in, head_pair, head_twin,
    tail_out, tail_in, tail_pair, tail_twin,
    left_out, left_in, right_out, right_in, col_mean,
    own_sem, z_send, z_recv, d_send, d_recv, p_send, p_recv, p_rest,
    x_send, x_recv,
):
    src_me, tgt_me = lax.axis_index("src"), lax.axis_index("tgt")
    x, y = src_me // NY, lax.rem(src_me, NY)
    z, core = tgt_me // 2, lax.rem(tgt_me, 2)
    row_blocks, col_blocks = sim.shape[0] // LANES, sim.shape[1] // LANES

    def around(v, step, n):
        return lax.rem(v + (step + n), n)

    def at_xy(dx, dy):
        return around(x, dx, NX) * NY + around(y, dy, NY)

    def at_z(dz):
        return around(z, dz, NZ) * 2 + core

    twin = (src_me, z * 2 + 1 - core)

    barrier = pltpu.get_barrier_semaphore()
    neighbours = [(src_me, at_z(1)), (src_me, at_z(-1)), twin]
    steps = ((1, 0), (-1, 0), (2, 0), (0, 1), (0, -1), (0, 2))
    neighbours += [(at_xy(*step), tgt_me) for step in steps]
    for device in neighbours:
        pl.semaphore_signal(barrier, inc=1, device_id=device, device_id_type=MESH)

    own = []
    for h in range(PIECES):
        part = pl.ds(h * 16, 16)
        own.append(pltpu.make_async_copy(src_ref.at[part], s_all.at[tgt_me, h], own_sem.at[0, h]))
    for h in range(QUARTERS):
        part = pl.ds(h * 16, 16)
        own.append(pltpu.make_async_copy(tgt_ref.at[part], t_all.at[src_me, h], own_sem.at[1, h]))
    for copy in own:
        copy.start()

    for copy in own:
        copy.wait()
    pl.semaphore_wait(barrier, len(neighbours))

    def z_copy(way, d, h, landed=False):
        step = 1 if way == 0 else -1
        slot = s_all.at[at_z(-step * (d if landed else d - 1)), h]
        return pltpu.make_async_remote_copy(
            src_ref=slot, dst_ref=slot,
            send_sem=z_send, recv_sem=z_recv.at[way, d - 1, h],
            device_id=(src_me, at_z(step)), device_id_type=MESH,
        )

    def piece(way, i):
        return (i + way * PIECES // 2) % PIECES

    def goes(d, i):
        return d < NZ // 2 or (d == NZ // 2 and i < PIECES // 2)

    def to_twin(dz, h):
        slot = s_all.at[at_z(dz), h]
        pltpu.make_async_remote_copy(
            src_ref=slot, dst_ref=slot, send_sem=d_send, recv_sem=d_recv.at[dz % NZ],
            device_id=twin, device_id_type=MESH,
        ).start()

    def from_twin(dz):
        slot = s_all.at[around(z, dz, NZ) * 2 + 1 - core]
        pltpu.make_async_remote_copy(
            src_ref=slot, dst_ref=slot, send_sem=d_send, recv_sem=d_recv.at[dz % NZ],
            device_id=twin, device_id_type=MESH,
        ).wait_recv()

    def z_event(d, i):
        for way in range(2):
            if goes(d, i):
                h = piece(way, i)
                z_copy(way, d, h, landed=True).wait_recv()
                if goes(d + 1, i):
                    z_copy(way, d + 1, h).start()
                to_twin(-d if way == 0 else d, h)

    def place(h, first, second):
        return at_xy(first, second) if h % 2 == 0 else at_xy(second, first)

    def p_copy(h, index, slice_at, move):
        slot = t_all.at[place(h, *slice_at), h]
        return pltpu.make_async_remote_copy(
            src_ref=slot, dst_ref=slot,
            send_sem=p_send, recv_sem=p_rest if index is None else p_recv.at[h, index],
            device_id=(place(h, *move), tgt_me), device_id_type=MESH,
        )

    up, down = (0, 1), (0, -1)
    offsets = (0, -1, 1, 2)
    upward = (True, False, False, False)

    def second(h, j):
        p_copy(h, 3 + j if upward[j] else None, (offsets[j], 0), up).start()
        p_copy(h, None if upward[j] else 3 + j, (offsets[j], 0), down).start()

    def below(h):
        p_copy(h, 0, (-1, 0), up).wait_recv()
        second(h, 1)

    def above(h):
        p_copy(h, 1, (1, 0), up).wait_recv()
        second(h, 2)

    def across(h):
        p_copy(h, 2, (2, 0), up).wait_recv()
        second(h, 3)

    def line(h, j):
        slice_at = (offsets[j], -1 if upward[j] else 1)
        p_copy(h, 3 + j, slice_at, up).wait_recv()
        p_copy(h, None, slice_at, up if upward[j] else down).start()

    for i in range(PIECES):
        for way in range(2):
            z_copy(way, 1, piece(way, i)).start()
    for h in range(QUARTERS):
        p_copy(h, 0, (0, 0), (1, 0)).start()
        p_copy(h, 1, (0, 0), (-1, 0)).start()
        p_copy(h, 2, (0, 0), (2, 0)).start()
    for h in range(QUARTERS):
        second(h, 0)
    for h in range(PIECES):
        to_twin(0, h)

    for b in range(row_blocks):
        scales = src_scale[:, b * LANES:(b + 1) * LANES]
        side[b * LANES:(b + 1) * LANES, :] = jnp.broadcast_to(scales, (LANES, LANES)).T
    columns[...] = jnp.full(columns.shape, LOW, F32)

    z_event(1, 0)
    for h in (0, 1):
        below(h)
        above(h)
    above(2)
    above(3)
    z_event(1, 1)
    across(0)
    z_event(1, 2)
    below(2)
    across(1)
    below(3)
    z_event(1, 3)
    line(0, 1)
    line(1, 1)
    z_event(2, 0)
    across(2)
    across(3)
    for h in (0, 1):
        line(h, 0)
    for h in (0, 1):
        line(h, 2)
    for h in (2, 3):
        line(h, 0)
    z_event(2, 1)
    for h in (2, 3):
        line(h, 2)
    line(0, 3)
    line(1, 3)
    z_event(2, 2)
    line(2, 1)
    line(3, 1)
    z_event(2, 3)
    line(2, 3)
    line(3, 3)
    for i in range(PIECES):
        z_event(3, i)
    pltpu.make_async_copy(t_all.at[pl.ds(0, 8)], t_all.at[pl.ds(0, 8)], p_rest).wait()

    def features(dz, part):
        return s_all[pl.ds(around(z, dz, NZ) * 2, 2), :, :, part].reshape(LANES, TILE)

    def targets(dz):
        return t_all[pl.ds(around(z, dz, NZ) * 2, 2)].reshape(LANES, sim.shape[1])

    def product(first, second, start, stop, fresh=False):
        @pl.loop(start, stop)
        def _(i):
            part = pl.ds(pl.multiple_of(i * TILE, TILE), TILE)
            left = jnp.concatenate([features(first, part), features(second, part)], axis=0)
            right = jnp.concatenate([targets(first), targets(second)], axis=0)
            dots = lax.dot_general(
                left, right, (((0,), (0,)), ((), ())), preferred_element_type=F32
            )
            if fresh:
                sim[part, :] = dots
            else:
                sim[part, :] = sim[part, :] + dots

    tiles = sim.shape[0] // TILE
    from_twin(-1)
    from_twin(1)
    product(-1, 1, 0, tiles, fresh=True)
    z_event(4, 0)
    from_twin(-2)
    from_twin(2)
    product(-2, 2, 0, tiles)
    z_event(4, 1)
    from_twin(-3)
    from_twin(3)
    product(-3, 3, 0, tiles)
    from_twin(0)
    from_twin(4)
    product(0, 4, 0, tiles)

    for slots, sem in ((s_all.at[pl.ds(0, 7)], z_send), (s_all.at[pl.ds(0, 8)], d_send),
                       (t_all.at[pl.ds(0, 15)], p_send)):
        pltpu.make_async_copy(slots, slots, sem).wait()

    out = (head_out, tail_out, left_out, right_out)
    into = (head_in, tail_in, left_in, right_in)

    def sweep(stage, change):
        def best_of_rows(b):
            def rows(g):
                return pl.ds(pl.multiple_of(b * LANES + g * 8, 8), 8)

            for g in range(16):
                beside = side[rows(g), :]
                values = []
                for c in range(col_blocks):
                    lane = pl.ds(c * LANES, LANES)
                    value = change(sim[rows(g), lane], beside, c)
                    sim[rows(g), lane] = value
                    values.append(value)
                best = merge4(sort4(values[:4]), sort4(values[4:]))
                for k in range(4):
                    lists[k, g * 8:(g + 1) * 8, :] = best[k]
            turned = [lists[k].T for k in range(4)]
            return over_sublanes(tree([[t[g * 8:(g + 1) * 8] for t in turned] for g in range(16)]))

        @pl.loop(0, 8, unroll=8)
        def _(b):
            best = best_of_rows(b)
            for k in range(4):
                head_out[pl.ds(8 * k + b, 1), :] = best[k][0:1]

        send(stage, HEAD)

        @pl.loop(8, row_blocks, unroll=4)
        def _(b):
            best = best_of_rows(b)
            for k in range(4):
                tail_out[pl.ds(QUAD[k] + b - 8, 1), :] = best[k][0:1]

        send(stage, TAIL)

        for part in (LEFT, RIGHT):
            first = 0 if part == LEFT else 4

            @pl.loop(0, row_blocks)
            def _(b, first=first):
                for c in range(first, first + 4):
                    lane = pl.ds(c * LANES, LANES)
                    quads = [
                        sort4([
                            sim[pl.ds(pl.multiple_of(b * LANES + (4 * q + g) * 8, 8), 8), lane]
                            for g in range(4)
                        ])
                        for q in range(4)
                    ]
                    best = merge4(tree(quads), [columns[c, k] for k in range(4)])
                    for k in range(4):
                        columns[c, k] = best[k]

            for c in range(4):
                best = over_sublanes([columns[first + c, k] for k in range(4)])
                for k in range(4):
                    out[part][QUAD[k] + c:QUAD[k] + c + 1, :] = best[k][0:1]
            send(stage, part)

    def send(stage, part):
        if part in (HEAD, TAIL):
            devices = [(src_me, at_z(r)) for r in (4, 3, 5, 2, 6, 1, 7)]
        else:
            steps = [(dx, dy) for dx in range(NX) for dy in range(NY) if dx or dy]
            steps.sort(key=lambda step: -sum(min(v, 4 - v) for v in step))
            devices = [(at_xy(*step), tgt_me) for step in steps]
        for slot, device in enumerate(devices):
            pltpu.make_async_remote_copy(
                src_ref=out[part], dst_ref=into[part].at[stage, slot],
                send_sem=x_send.at[part], recv_sem=x_recv.at[stage, part],
                device_id=device, device_id_type=MESH,
            ).start()

    def gathered(stage, part):
        slots = into[part].at[stage]
        pltpu.make_async_copy(slots, slots, x_recv.at[stage, part]).wait()
        load = load8 if part == HEAD else load4
        count = into[part].shape[1]
        best = tree([load(out[part])] + [load(into[part].at[stage, r]) for r in range(count)])
        return best

    def sent(stage):
        for part in (HEAD, TAIL, LEFT, RIGHT):
            slots = into[part].at[stage]
            pltpu.make_async_copy(slots, slots, x_send.at[part]).wait()

    def twin_copy(stage, part):
        mine, theirs = ((head_pair, head_twin), (tail_pair, tail_twin))[part]
        return pltpu.make_async_remote_copy(
            src_ref=mine, dst_ref=theirs.at[stage],
            send_sem=x_send.at[4 + part], recv_sem=x_recv.at[stage, 4 + part],
            device_id=twin, device_id_type=MESH,
        )

    def combined(stage, use_head, use_tail, use_cols):
        head = gathered(stage, HEAD)
        store8(head_pair, head)
        twin_copy(stage, HEAD).start()
        tail = gathered(stage, TAIL)
        store4(tail_pair, tail)
        twin_copy(stage, TAIL).start()
        use_cols(0, gathered(stage, LEFT))
        twin_copy(stage, HEAD).wait_recv()
        use_head(merge4(head, load8(head_twin.at[stage])))
        twin_copy(stage, TAIL).wait_recv()
        use_tail(merge4(tail, load4(tail_twin.at[stage])))
        use_cols(4, gathered(stage, RIGHT))
        for part in (HEAD, TAIL):
            twin_copy(stage, part).wait_send()
        sent(stage)

    def scaled(value, beside, c):
        return value * beside * tgt_scale[:, c * LANES:(c + 1) * LANES]

    def half_mean(best):
        return (best[0] + best[1] + best[2] + best[3]) * 0.125

    def rows_mean(first, count):
        def use(best):
            mean = half_mean(best)
            for b in range(count):
                at = (first + b) * LANES
                side[at:at + LANES, :] = jnp.broadcast_to(mean[b:b + 1], (LANES, LANES)).T
        return use

    def cols_mean(first, best):
        mean = half_mean(best)
        for c in range(4):
            col_mean[first + c] = jnp.broadcast_to(mean[c:c + 1], (8, LANES))

    sweep(0, scaled)
    combined(0, rows_mean(0, 8), rows_mean(8, row_blocks - 8), cols_mean)

    columns[...] = jnp.full(columns.shape, LOW, F32)

    def margin(value, beside, c):
        return value / (beside + col_mean[c])

    def rows_out(first, count):
        def use(best):
            for k in range(4):
                for b in range(count):
                    at = (first + b) * LANES
                    fwd_ref[k:k + 1, at:at + LANES] = best[k][b:b + 1]
        return use

    def cols_out(first, best):
        for k in range(4):
            for c in range(4):
                at = (first + c) * LANES
                bwd_ref[k:k + 1, at:at + LANES] = best[k][c:c + 1]

    sweep(1, margin)
    combined(1, rows_out(0, 8), rows_out(8, row_blocks - 8), cols_out)


def body(src_codes, src_scale, tgt_codes, tgt_scale):
    depth, rows = src_codes.shape
    cols = tgt_codes.shape[1]
    col_blocks = cols // LANES
    vmem = pl.BlockSpec(memory_space=pltpu.VMEM)
    hbm = pl.BlockSpec(memory_space=pltpu.HBM)
    dma = pltpu.SemaphoreType.DMA
    return pl.pallas_call(
        kernel,
        out_shape=(
            jax.ShapeDtypeStruct((4, rows), F32),
            jax.ShapeDtypeStruct((4, cols), F32),
        ),
        in_specs=[hbm, vmem, hbm, vmem],
        out_specs=(vmem, vmem),
        scratch_shapes=[
            pltpu.VMEM((GROUP, PIECES, depth // PIECES, rows), jnp.bfloat16),
            pltpu.VMEM((GROUP, QUARTERS, depth // QUARTERS, cols), jnp.bfloat16),
            pltpu.VMEM((rows, cols), F32),
            pltpu.VMEM((rows, LANES), F32),
            pltpu.VMEM((4, LANES, LANES), F32),
            pltpu.VMEM((col_blocks, 4, 8, LANES), F32),
            pltpu.VMEM((32, LANES), F32),
            pltpu.VMEM((2, NZ - 1, 32, LANES), F32),
            pltpu.VMEM((32, LANES), F32),
            pltpu.VMEM((2, 32, LANES), F32),
            pltpu.VMEM((16, LANES), F32),
            pltpu.VMEM((2, NZ - 1, 16, LANES), F32),
            pltpu.VMEM((16, LANES), F32),
            pltpu.VMEM((2, 16, LANES), F32),
            pltpu.VMEM((16, LANES), F32),
            pltpu.VMEM((2, GROUP - 1, 16, LANES), F32),
            pltpu.VMEM((16, LANES), F32),
            pltpu.VMEM((2, GROUP - 1, 16, LANES), F32),
            pltpu.VMEM((col_blocks, 8, LANES), F32),
            dma((2, 4)),
            dma,
            dma((2, NZ // 2, PIECES)),
            dma,
            dma((NZ,)),
            dma,
            dma((QUARTERS, 7)),
            dma,
            dma((6,)),
            dma((2, 6)),
        ],
        compiler_params=pltpu.CompilerParams(
            collective_id=0, has_side_effects=True, vmem_limit_bytes=55150 * 1024
        ),
        name="mine",
    )(src_codes, src_scale.reshape(1, rows), tgt_codes, tgt_scale.reshape(1, cols))


def solution(mesh):
    placed = (P("tgt", "src"), P("src"), P("src", "tgt"), P("tgt"))
    return jax.shard_map(
        body,
        mesh=mesh,
        in_specs=placed,
        out_specs=(P(None, "src"), P(None, "tgt")),
        check_vma=False,
    )
```
